32 devices in a mesh: bins: 4 (over y, core), space: 8 (over z, x).
Axes of the slice: x: 2, y: 2, z: 4, core: 2. Of those that a mesh axis runs over, the one named last changes fastest.
Arguments:
- spectra: float32 [1152, 512, 128], P('bins', 'space'), may hold values from 0.05 to 2
- land_mask: int32 [512, 128], P('space'), may hold values 0 or 1
- growth: float32 [1152], replicated, may hold values from 0.1 to 1
- band_weight: float32 [1152], replicated, may hold values from 0.00043402778 to 0.0034722222
- kernel_gain: bfloat16 [1152, 1152], replicated, may hold values from -0.1875 to 0.1875
- kernel_loss: bfloat16 [1152, 1152], replicated, may hold values from -0.1875 to 0.1875
Outputs:
- updated: float32 [1152, 512, 128], P('bins', 'space')
The draws below stay inside these ranges and needn't reach their ends.
All inputs are finite; a program needn't handle non-finite values. No bound on the sum of `land_mask` on one device may be relied on, other than what follows from the above.
Results may differ from the reference program's by a relative error of at most 0.00056.
Values sent between devices are 32-bit elements; how exact they have to be, the bound alone decides.
No kernel may reach another device: no remote copies, remote signals or barrier semaphores. Data moves between devices by JAX's collectives and lax.ppermute only.
A program may use at most 64 MiB of HBM per device.

```python
import math
import jax
import jax.numpy as jnp
from jax import lax

NF = 32
ND = 36
NB = 1152
CX = 64
NY = 128
SUBSTEPS = 4
NX = 512
N_SPACE = 8


def plant(array, key, low, largest):
    shape = array.shape
    place = [jax.random.randint(jax.random.fold_in(key, axis), (), 0, shape[axis]) for axis in range(len(shape))]
    array = array.at[tuple(place)].set(low)
    longest = shape.index(max(shape))
    place[longest] = (place[longest] + 1) % shape[longest]
    return array.at[tuple(place)].set(largest)


def steps_of(stream_key, extent, cuts, smallest, high):
    def one(axis_at, blocks):
        steps = jax.random.uniform(jax.random.fold_in(jax.random.fold_in(stream_key, 6), axis_at), (blocks,), jnp.float32, smallest / len(cuts), high / len(cuts))
        return jnp.repeat(jnp.exp(steps), extent[axis_at] // blocks).reshape((-1,) + (1,) * (len(extent) - axis_at - 1))

    level = one(*cuts[0])
    for cut in cuts[1:]:
        level = level * one(*cut)
    return level


def normal_values(stream_key, dims, spread, limit, held_as=jnp.bfloat16):
    entries = jax.random.normal(stream_key, dims, jnp.float32) * spread
    return jnp.minimum(jnp.maximum(entries, -limit), limit).astype(held_as)


def setup_inputs(seed: int = 0) -> dict:
    splits = jax.random.split(jax.random.key(seed), 7)
    return {
        "spectra": jnp.clip(jnp.exp(math.log(2.0) - 3.6888794 * jax.random.uniform(splits[0], (NB, NX, NY), jnp.float32) ** steps_of(splits[0], (NB, NX, NY), ((0, 4), (1, 8)), -0.2, 0.2)), 0.05, 2.0),
        "land_mask": plant((jax.random.randint(splits[1], (NX, NY), 0, 4) < 3).astype(jnp.int32), jax.random.fold_in(splits[1], 1), 0, 1),
        "growth": jnp.clip(jnp.exp(jax.random.uniform(splits[2], (NB,), jnp.float32, math.log(0.1), math.log(1.0))), 0.1, 1.0),
        "band_weight": jnp.clip(jnp.exp(jax.random.uniform(splits[3], (NB,), jnp.float32, math.log(0.00043402778), math.log(0.0034722222))), 0.00043402778, 0.0034722222),
        "kernel_gain": normal_values(splits[4], (NB, NB), NB ** -0.5, 0.1875),
        "kernel_loss": normal_values(splits[5], (NB, NB), NB ** -0.5, 0.1875),
    }


def courants():
    index = jnp.arange(NB, dtype=jnp.int32)
    freq = (index // ND).astype(jnp.float32)
    direc = (index % ND).astype(jnp.float32)
    group = 1.0 / (1.0 + 2.3 * freq / max(NF - 1, 1))
    theta = 2.0 * math.pi * (direc + 0.5) / ND
    return 0.9 * group * jnp.cos(theta), 0.9 * group * jnp.sin(theta)


def upwind(field, speed, axis):
    plus = jnp.maximum(speed, 0.0)
    minus = jnp.maximum(-speed, 0.0)
    count = field.shape[axis]
    widths = [(0, 0)] * field.ndim
    widths[axis] = (1, 1)
    padded = jnp.pad(field, widths)
    lower = lax.slice_in_dim(padded, 0, count, axis=axis)
    upper = lax.slice_in_dim(padded, 2, count + 2, axis=axis)
    return field - plus * (field - lower) - minus * (field - upper)


def sources(block, growth, band_weight, kernel_gain, kernel_loss):
    state = block.astype(jnp.bfloat16)
    square = (block * block).astype(jnp.bfloat16)
    gain = jnp.dot(kernel_gain, state, preferred_element_type=jnp.float32)
    loss = jnp.dot(kernel_loss, square, preferred_element_type=jnp.float32)
    energy = jnp.sum(band_weight[:, None] * block, axis=0)
    return (block + 0.25 * (growth[:, None] * block + block * gain - loss)) / (1.0 + 0.5 * energy)


def reference(spectra, land_mask, growth, band_weight, kernel_gain, kernel_loss):
    speed_x, speed_y = courants()
    sea = land_mask.astype(jnp.float32)
    field = spectra
    for step in range(SUBSTEPS):
        field = upwind(field, speed_x[:, None, None], 1)
        field = upwind(field, speed_y[:, None, None], 2)
        field = sea[None] * field
    blocks = field.reshape(NB, N_SPACE, CX * NY).transpose(1, 0, 2)
    result = lax.map(lambda block: sources(block, growth, band_weight, kernel_gain, kernel_loss), blocks)
    result = result.transpose(1, 0, 2).reshape(NB, NX, NY)
    return sea[None] * result
```

```python
import functools
import math

import jax
import jax.numpy as jnp
from jax import lax
from jax.experimental import pallas as pl
from jax.experimental.pallas import tpu as pltpu
from jax.sharding import PartitionSpec as P

NF = 32
ND = 36
SUBSTEPS = 4
TILE = 8
LANES = 128


def courants(first, count):
    index = first + jnp.arange(count, dtype=jnp.int32)
    freq = (index // ND).astype(jnp.float32)
    direc = (index % ND).astype(jnp.float32)
    group = 1.0 / (1.0 + 2.3 * freq / max(NF - 1, 1))
    theta = 2.0 * math.pi * (direc + 0.5) / ND
    return (0.9 * group * jnp.cos(theta), 0.9 * group * jnp.sin(theta))


def pick(count, options):
    for parts in options:
        if count % (parts * TILE) == 0:
            return parts
    return 1


def edge_kernel(low_ref, high_ref, low_mask, high_mask, head_ref, tail_ref):
    bins = low_ref.shape[0]
    low = low_ref.reshape(bins * TILE, LANES)
    high = high_ref.reshape(bins * TILE, LANES)
    for row in range(SUBSTEPS):
        behind = TILE - SUBSTEPS + row
        head_ref[row, pl.ds(0, bins), :] = low[pl.ds(row, bins, stride=TILE), :]
        tail_ref[row, pl.ds(0, bins), :] = high[pl.ds(behind, bins, stride=TILE), :]
        sea_low = low_mask[pl.ds(row, 1), :].astype(jnp.float32)
        sea_high = high_mask[pl.ds(behind, 1), :].astype(jnp.float32)
        head_ref[row, pl.ds(bins, TILE), :] = jnp.broadcast_to(sea_low, (TILE, LANES))
        tail_ref[row, pl.ds(bins, TILE), :] = jnp.broadcast_to(sea_high, (TILE, LANES))


def edges(spectra, land_mask):
    bins, rows, columns = spectra.shape
    last = rows // TILE - 1
    shape = jax.ShapeDtypeStruct((SUBSTEPS, bins + TILE, columns), jnp.float32)
    whole = pl.BlockSpec((SUBSTEPS, bins + TILE, columns), lambda i: (0, 0, 0))
    return pl.pallas_call(
        edge_kernel,
        grid=(1,),
        in_specs=[
            pl.BlockSpec((bins, TILE, columns), lambda i: (0, 0, 0)),
            pl.BlockSpec((bins, TILE, columns), lambda i: (0, last, 0)),
            pl.BlockSpec((TILE, columns), lambda i: (0, 0)),
            pl.BlockSpec((TILE, columns), lambda i: (last, 0)),
        ],
        out_specs=[whole, whole],
        out_shape=[shape, shape],
        name="edges",
    )(spectra, spectra, land_mask, land_mask)


def propagate_kernel(first, last, *refs):
    if first:
        halo_ref, mid_ref, next_ref, mid_mask, next_mask = refs[:5]
        halo_mask = refs[5]
        rest = refs[6:]
    elif last:
        prev_ref, mid_ref, halo_ref, prev_mask, mid_mask = refs[:5]
        halo_mask = refs[5]
        rest = refs[6:]
    else:
        prev_ref, mid_ref, next_ref, prev_mask, mid_mask, next_mask = refs[:6]
        rest = refs[6:]
    cx_ref, cy_ref, out_ref, sea_scr = rest
    bins = mid_ref.shape[0]
    window = TILE + 2 * SUBSTEPS

    def sea_row(k):
        if k < SUBSTEPS:
            if first:
                return halo_mask[k, pl.ds(0, 1), :]
            return prev_mask[pl.ds(TILE - SUBSTEPS + k, 1), :].astype(jnp.float32)
        if k < SUBSTEPS + TILE:
            return mid_mask[pl.ds(k - SUBSTEPS, 1), :].astype(jnp.float32)
        if last:
            return halo_mask[k - SUBSTEPS - TILE, pl.ds(0, 1), :]
        return next_mask[pl.ds(k - SUBSTEPS - TILE, 1), :].astype(jnp.float32)

    for k in range(window):
        sea_scr[k] = jnp.broadcast_to(sea_row(k), (TILE, LANES))

    mid = mid_ref.reshape(bins * TILE, LANES)
    before = None if first else prev_ref.reshape(bins * TILE, LANES)
    after = None if last else next_ref.reshape(bins * TILE, LANES)
    lane = lax.broadcasted_iota(jnp.int32, (TILE, LANES), 1)

    def body(tile, carry):
        base = pl.multiple_of(tile * TILE, TILE)
        origin = tile * (TILE * TILE)
        cx = cx_ref[pl.ds(base, TILE), :]
        cy = cy_ref[pl.ds(base, TILE), :]
        ax = jnp.abs(cx)
        ay = jnp.abs(cy)
        east = cx > 0.0
        from_left = (cy > 0.0) & (lane > 0)
        from_right = (cy <= 0.0) & (lane < LANES - 1)

        def load(k):
            if k < SUBSTEPS:
                if first:
                    return halo_ref[k, pl.ds(base, TILE), :]
                return before[pl.ds(origin + TILE - SUBSTEPS + k, TILE, stride=TILE), :]
            if k < SUBSTEPS + TILE:
                return mid[pl.ds(origin + k - SUBSTEPS, TILE, stride=TILE), :]
            if last:
                return halo_ref[k - SUBSTEPS - TILE, pl.ds(base, TILE), :]
            return after[pl.ds(origin + k - SUBSTEPS - TILE, TILE, stride=TILE), :]

        field = [load(k) for k in range(window)]
        for step in range(SUBSTEPS):
            start = step + 1
            fresh = []
            for k in range(start, window - start):
                here = k - step
                value = field[here]
                source = jnp.where(east, field[here - 1], field[here + 1])
                value = value - ax * (value - source)
                left = pltpu.roll(value, 1, 1)
                right = pltpu.roll(value, LANES - 1, 1)
                source = jnp.where(from_left, left, jnp.where(from_right, right, 0.0))
                value = value - ay * (value - source)
                fresh.append(sea_scr[k] * value)
            field = fresh
        for row in range(TILE):
            out_ref[row, pl.ds(base, TILE), :] = field[row]
        return carry

    lax.fori_loop(0, bins // TILE, body, 0)


def propagate(spectra, land_mask, cx, cy, block, halo):
    bins, rows, columns = spectra.shape
    last_block = rows // TILE - 1
    first, last = block == 0, block == last_block
    parts = pick(bins, (3, 2))
    size = bins // parts

    def cells(at):
        return pl.BlockSpec((size, TILE, columns), lambda i: (i, at, 0))

    def sea(at):
        return pl.BlockSpec((TILE, columns), lambda i: (at, 0))

    edge = pl.BlockSpec((SUBSTEPS, size, columns), lambda i: (0, i, 0))
    edge_sea = pl.BlockSpec((SUBSTEPS, TILE, columns), lambda i: (0, bins // TILE, 0))
    if first:
        specs = [edge, cells(0), cells(1), sea(0), sea(1), edge_sea]
        args = [halo, spectra, spectra, land_mask, land_mask, halo]
    elif last:
        specs = [cells(block - 1), cells(block), edge, sea(block - 1), sea(block), edge_sea]
        args = [spectra, spectra, halo, land_mask, land_mask, halo]
    else:
        specs = [cells(block - 1), cells(block), cells(block + 1)]
        specs += [sea(block - 1), sea(block), sea(block + 1)]
        args = [spectra] * 3 + [land_mask] * 3
    speed = pl.BlockSpec((size, columns), lambda i: (i, 0))
    return pl.pallas_call(
        functools.partial(propagate_kernel, first, last),
        grid=(parts,),
        in_specs=specs + [speed, speed],
        out_specs=pl.BlockSpec((TILE, size, columns), lambda i: (0, i, 0)),
        out_shape=jax.ShapeDtypeStruct((TILE, bins, columns), jnp.float32),
        scratch_shapes=[pltpu.VMEM((TILE + 2 * SUBSTEPS, TILE, columns), jnp.float32)],
        name="propagate",
    )(*args, cx, cy)


PAIR = 2


def source_kernel(count, aliased, where_ref, *refs):
    fields = refs[:count]
    gain_ref, loss_ref, growth_ref, weight_ref, mask_ref = refs[count : count + 5]
    rest = refs[count + 5 :]
    if aliased:
        rest = rest[1:]
    out_ref, state, square = rest
    bins = fields[0].shape[1]
    step = pl.program_id(0)
    energy = [jnp.zeros((TILE, LANES), jnp.float32) for _ in range(PAIR)]
    for n in range(count):
        place = pl.multiple_of(where_ref[n] * bins, 16)
        for row in range(PAIR):
            value = fields[n][row]
            state[pl.ds(place, bins), pl.ds(row * LANES, LANES)] = value.astype(jnp.bfloat16)
            square[pl.ds(place, bins), pl.ds(row * LANES, LANES)] = (value * value).astype(jnp.bfloat16)
            weighted = weight_ref[pl.ds(place, bins), :] * value
            energy[row] = energy[row] + jnp.sum(weighted.reshape(bins // TILE, TILE, LANES), axis=0)
    gain = jnp.dot(gain_ref[...], state[...], preferred_element_type=jnp.float32)
    loss = jnp.dot(loss_ref[...], square[...], preferred_element_type=jnp.float32)
    out = out_ref.reshape(bins * TILE, LANES)
    for row in range(PAIR):
        at = step * PAIR + row
        total = jnp.sum(energy[row], axis=0, keepdims=True)
        sea = mask_ref[pl.ds(at, 1), :].astype(jnp.float32)
        scale = sea / (1.0 + 0.5 * total)
        value = fields[0][row]
        grown = growth_ref[...] * value
        part = slice(row * LANES, (row + 1) * LANES)
        fresh = (value + 0.25 * (grown + value * gain[:, part] - loss[:, part])) * scale
        out[pl.ds(at, bins, stride=TILE), :] = fresh


def add_sources(where, fields, kernels, growth, weight, land_mask, block, out, shape):
    count = len(fields)
    bins, rows, columns = shape
    every = weight.shape[0]
    cells = pl.BlockSpec((PAIR, bins, columns), lambda i, w: (i, 0, 0))
    table = pl.BlockSpec((bins, every), lambda i, w: (w[0], 0))
    specs = [cells] * count + [
        table,
        table,
        pl.BlockSpec((bins, columns), lambda i, w: (0, 0)),
        pl.BlockSpec((every, columns), lambda i, w: (0, 0)),
        pl.BlockSpec((TILE, columns), lambda i, w: (block, 0)),
    ]
    args = [*fields, *kernels, growth, weight, land_mask]
    aliases = {}
    if out is not None:
        specs.append(pl.BlockSpec(memory_space=pl.ANY))
        args.append(out)
        aliases = {len(args): 0}
    return pl.pallas_call(
        functools.partial(source_kernel, count, out is not None),
        grid_spec=pltpu.PrefetchScalarGridSpec(
            num_scalar_prefetch=1,
            grid=(TILE // PAIR,),
            in_specs=specs,
            out_specs=pl.BlockSpec((bins, TILE, columns), lambda i, w: (0, block, 0)),
            scratch_shapes=[
                pltpu.VMEM((every, PAIR * columns), jnp.bfloat16),
                pltpu.VMEM((every, PAIR * columns), jnp.bfloat16),
            ],
        ),
        out_shape=jax.ShapeDtypeStruct(shape, jnp.float32),
        input_output_aliases=aliases,
        name="sources",
    )(where, *args)


def local(spectra, land_mask, growth, band_weight, kernel_gain, kernel_loss):
    bins, rows, columns = spectra.shape
    every = band_weight.shape[0]
    me = lax.axis_index("bins")
    group = lax.axis_size("bins")
    slabs = lax.axis_size("space")
    chips = group // 2
    speed_x, speed_y = courants(me * bins, bins)
    cx = jnp.broadcast_to(speed_x[:, None], (bins, columns))
    cy = jnp.broadcast_to(speed_y[:, None], (bins, columns))
    mine = lax.dynamic_slice_in_dim(growth, me * bins, bins)
    growth_wide = jnp.broadcast_to(mine[:, None], (bins, columns))
    weight_wide = jnp.broadcast_to(band_weight[:, None], (every, columns))

    partner = [(i, i ^ 1) for i in range(group)]
    shifts = [[(i, (i + 2 * s) % group) for i in range(group)] for s in range(1, chips)]
    came = [(me + group - 2 * s) % group for s in range(1, chips)]
    where = [me, me ^ 1]
    for source in came:
        where += [source, source ^ 1]
    where = jnp.stack(where).astype(jnp.int32)

    blocks = rows // TILE
    order = list(range(1, blocks - 1)) + [0, blocks - 1]
    head, tail = edges(spectra, land_mask)
    before = lax.ppermute(tail, "space", [(i, i + 1) for i in range(slabs - 1)])
    after = lax.ppermute(head, "space", [(i + 1, i) for i in range(slabs - 1)])

    fields = {}
    for block in order:
        halo = before if block == 0 else after if block == blocks - 1 else None
        fields[block] = propagate(spectra, land_mask, cx, cy, block, halo)
    far = {b: [lax.ppermute(fields[b], "bins", s) for s in shifts] for b in order}
    near = {b: lax.ppermute(fields[b], "bins", partner) for b in order}
    out = None
    for block in order:
        direct = far[block]
        if out is not None:
            direct, out = lax.optimization_barrier((direct, out))
        parts = [fields[block], near[block]]
        for came_in in direct:
            parts += [came_in, lax.ppermute(came_in, "bins", partner)]
        kernels = (kernel_gain, kernel_loss)
        out = add_sources(where, parts, kernels, growth_wide, weight_wide, land_mask, block, out, spectra.shape)
    return out


def solution(mesh):
    in_specs = (P("bins", "space", None), P("space", None), P(), P(), P(), P())
    out_specs = P("bins", "space", None)
    return jax.shard_map(local, mesh=mesh, in_specs=in_specs, out_specs=out_specs, check_vma=False)
```

```python
import functools
import math

import jax
import jax.numpy as jnp
from jax import lax
from jax.experimental import pallas as pl
from jax.experimental.pallas import tpu as pltpu
from jax.sharding import PartitionSpec as P


NF = 32
ND = 36
SUBSTEPS = 4
TILE = 8
LANES = 128


def courants(first, count):
    index = first + jnp.arange(count, dtype=jnp.int32)
    freq = (index // ND).astype(jnp.float32)
    direc = (index % ND).astype(jnp.float32)
    group = 1.0 / (1.0 + 2.3 * freq / max(NF - 1, 1))
    theta = 2.0 * math.pi * (direc + 0.5) / ND
    return (0.9 * group * jnp.cos(theta), 0.9 * group * jnp.sin(theta))


def pick(count, options):
    for parts in options:
        if count % (parts * TILE) == 0:
            return parts
    return 1


def edge_kernel(low_ref, high_ref, low_mask, high_mask, head_ref, tail_ref):
    bins = low_ref.shape[0]
    low = low_ref.reshape(bins * TILE, LANES)
    high = high_ref.reshape(bins * TILE, LANES)
    for row in range(SUBSTEPS):
        behind = TILE - SUBSTEPS + row
        head_ref[row, pl.ds(0, bins), :] = low[pl.ds(row, bins, stride=TILE), :]
        tail_ref[row, pl.ds(0, bins), :] = high[pl.ds(behind, bins, stride=TILE), :]
        sea_low = low_mask[pl.ds(row, 1), :].astype(jnp.float32)
        sea_high = high_mask[pl.ds(behind, 1), :].astype(jnp.float32)
        head_ref[row, pl.ds(bins, TILE), :] = jnp.broadcast_to(sea_low, (TILE, LANES))
        tail_ref[row, pl.ds(bins, TILE), :] = jnp.broadcast_to(sea_high, (TILE, LANES))


def edges(spectra, land_mask):
    bins, rows, columns = spectra.shape
    last = rows // TILE - 1
    shape = jax.ShapeDtypeStruct((SUBSTEPS, bins + TILE, columns), jnp.float32)
    whole = pl.BlockSpec((SUBSTEPS, bins + TILE, columns), lambda i: (0, 0, 0))
    return pl.pallas_call(
        edge_kernel,
        grid=(1,),
        in_specs=[
            pl.BlockSpec((bins, TILE, columns), lambda i: (0, 0, 0)),
            pl.BlockSpec((bins, TILE, columns), lambda i: (0, last, 0)),
            pl.BlockSpec((TILE, columns), lambda i: (0, 0)),
            pl.BlockSpec((TILE, columns), lambda i: (last, 0)),
        ],
        out_specs=[whole, whole],
        out_shape=[shape, shape],
        name="edges",
    )(spectra, spectra, land_mask, land_mask)


def fill_sea(first, last, prev_mask, mid_mask, next_mask, halo_mask, sea_scr):
    for k in range(TILE + 2 * SUBSTEPS):
        if k < SUBSTEPS:
            if first:
                row = halo_mask[k, pl.ds(0, 1), :]
            else:
                row = prev_mask[pl.ds(TILE - SUBSTEPS + k, 1), :].astype(jnp.float32)
        elif k < SUBSTEPS + TILE:
            row = mid_mask[pl.ds(k - SUBSTEPS, 1), :].astype(jnp.float32)
        elif last:
            row = halo_mask[k - SUBSTEPS - TILE, pl.ds(0, 1), :]
        else:
            row = next_mask[pl.ds(k - SUBSTEPS - TILE, 1), :].astype(jnp.float32)
        sea_scr[k] = jnp.broadcast_to(row, (TILE, LANES))


def propagate_kernel(first, last, *refs):
    halo_ref = halo_mask = prev_ref = prev_mask = next_ref = next_mask = None
    if first:
        halo_ref, mid_ref, next_ref, mid_mask, next_mask, halo_mask = refs[:6]
    elif last:
        prev_ref, mid_ref, halo_ref, prev_mask, mid_mask, halo_mask = refs[:6]
    else:
        prev_ref, mid_ref, next_ref, prev_mask, mid_mask, next_mask = refs[:6]
    cx_ref, cy_ref, out_ref, sea_scr = refs[6:]
    fill_sea(first, last, prev_mask, mid_mask, next_mask, halo_mask, sea_scr)
    bins = mid_ref.shape[0]
    window = TILE + 2 * SUBSTEPS

    mid = mid_ref.reshape(bins * TILE, LANES)
    before = None if first else prev_ref.reshape(bins * TILE, LANES)
    after = None if last else next_ref.reshape(bins * TILE, LANES)
    lane = lax.broadcasted_iota(jnp.int32, (TILE, LANES), 1)

    def body(tile, carry):
        base = pl.multiple_of(tile * TILE, TILE)
        origin = tile * (TILE * TILE)
        cx = cx_ref[pl.ds(base, TILE), :]
        cy = cy_ref[pl.ds(base, TILE), :]
        ax = jnp.abs(cx)
        ay = jnp.abs(cy)
        east = cx > 0.0
        from_left = (cy > 0.0) & (lane > 0)
        from_right = (cy <= 0.0) & (lane < LANES - 1)

        def load(k):
            if k < SUBSTEPS:
                if first:
                    return halo_ref[k, pl.ds(base, TILE), :]
                return before[pl.ds(origin + TILE - SUBSTEPS + k, TILE, stride=TILE), :]
            if k < SUBSTEPS + TILE:
                return mid[pl.ds(origin + k - SUBSTEPS, TILE, stride=TILE), :]
            if last:
                return halo_ref[k - SUBSTEPS - TILE, pl.ds(base, TILE), :]
            return after[pl.ds(origin + k - SUBSTEPS - TILE, TILE, stride=TILE), :]

        field = [load(k) for k in range(window)]
        for step in range(SUBSTEPS):
            start = step + 1
            fresh = []
            for k in range(start, window - start):
                here = k - step
                value = field[here]
                source = jnp.where(east, field[here - 1], field[here + 1])
                value = value - ax * (value - source)
                left = pltpu.roll(value, 1, 1)
                right = pltpu.roll(value, LANES - 1, 1)
                source = jnp.where(from_left, left, jnp.where(from_right, right, 0.0))
                value = value - ay * (value - source)
                fresh.append(sea_scr[k] * value)
            field = fresh
        for row in range(TILE):
            out_ref[row, pl.ds(base, TILE), :] = field[row]
        return carry

    lax.fori_loop(0, bins // TILE, body, 0)


def sorted_kernel(first, last, *refs):
    halo_ref = halo_mask = prev_ref = prev_mask = next_ref = next_mask = None
    if first:
        halo_ref, mid_ref, next_ref, mid_mask, next_mask, halo_mask = refs[:6]
    elif last:
        prev_ref, mid_ref, halo_ref, prev_mask, mid_mask, halo_mask = refs[:6]
    else:
        prev_ref, mid_ref, next_ref, prev_mask, mid_mask, next_mask = refs[:6]
    cx_ref, cy_ref, out_ref, sea_scr = refs[6:]
    fill_sea(first, last, prev_mask, mid_mask, next_mask, halo_mask, sea_scr)
    bins = mid_ref.shape[0]
    flat = bins * TILE
    mid = mid_ref.reshape(flat, LANES)
    before = None if first else prev_ref.reshape(flat, LANES)
    after = None if last else next_ref.reshape(flat, LANES)
    lane = lax.broadcasted_iota(jnp.int32, (TILE, LANES), 1)
    quarter = ND // 4
    far = ND * TILE

    def body(turn, carry):
        for quadrant in range(4):
            direction = quadrant * quarter + turn
            comb = pl.ds(direction, TILE, stride=ND)
            east = quadrant in (0, 3)
            north = quadrant in (0, 1)
            ax = jnp.abs(cx_ref[comb, :])
            ay = jnp.abs(cy_ref[comb, :])
            keep = 1.0 - ay
            edge = lane == (0 if north else LANES - 1)
            take = jnp.where(edge, 0.0, ay)

            def cells(ref, row):
                return ref[pl.ds(direction * TILE + row, TILE, stride=far), :]

            inner = [cells(mid, row) for row in range(TILE)]
            if east:
                if first:
                    outer = [halo_ref[row, comb, :] for row in range(SUBSTEPS)]
                else:
                    outer = [cells(before, TILE - SUBSTEPS + row) for row in range(SUBSTEPS)]
                field = outer + inner
            else:
                if last:
                    outer = [halo_ref[row, comb, :] for row in range(SUBSTEPS)]
                else:
                    outer = [cells(after, row) for row in range(SUBSTEPS)]
                field = inner + outer
            for step in range(SUBSTEPS):
                fresh = []
                for k in range(len(field) - 1):
                    if east:
                        value, source, at = field[k + 1], field[k], step + 1 + k
                    else:
                        value, source, at = field[k], field[k + 1], SUBSTEPS + k
                    value = value - ax * (value - source)
                    aside = pltpu.roll(value, 1 if north else LANES - 1, 1)
                    fresh.append(sea_scr[at] * (keep * value + take * aside))
                field = fresh
            for row in range(TILE):
                out_ref[row, comb, :] = field[row]
        return carry

    lax.fori_loop(0, quarter, body, 0)


def propagate(spectra, land_mask, cx, cy, block, halo):
    bins, rows, columns = spectra.shape
    last_block = rows // TILE - 1
    first, last = block == 0, block == last_block
    by_direction = bins == TILE * ND and ND % 4 == 0
    parts = 1 if by_direction else pick(bins, (3, 2))
    kernel = sorted_kernel if by_direction else propagate_kernel
    size = bins // parts

    def cells(at):
        return pl.BlockSpec((size, TILE, columns), lambda i: (i, at, 0))

    def sea(at):
        return pl.BlockSpec((TILE, columns), lambda i: (at, 0))

    edge = pl.BlockSpec((SUBSTEPS, size, columns), lambda i: (0, i, 0))
    edge_sea = pl.BlockSpec((SUBSTEPS, TILE, columns), lambda i: (0, bins // TILE, 0))
    if first:
        specs = [edge, cells(0), cells(1), sea(0), sea(1), edge_sea]
        args = [halo, spectra, spectra, land_mask, land_mask, halo]
    elif last:
        specs = [cells(block - 1), cells(block), edge, sea(block - 1), sea(block), edge_sea]
        args = [spectra, spectra, halo, land_mask, land_mask, halo]
    else:
        specs = [cells(block - 1), cells(block), cells(block + 1)]
        specs += [sea(block - 1), sea(block), sea(block + 1)]
        args = [spectra] * 3 + [land_mask] * 3
    speed = pl.BlockSpec((size, columns), lambda i: (i, 0))
    return pl.pallas_call(
        functools.partial(kernel, first, last),
        grid=(parts,),
        in_specs=specs + [speed, speed],
        out_specs=pl.BlockSpec((TILE, size, columns), lambda i: (0, i, 0)),
        out_shape=jax.ShapeDtypeStruct((TILE, bins, columns), jnp.float32),
        scratch_shapes=[pltpu.VMEM((TILE + 2 * SUBSTEPS, TILE, columns), jnp.float32)],
        name="propagate",
    )(*args, cx, cy)


PAIR = 2


def source_kernel(count, aliased, where_ref, *refs):
    fields = refs[:count]
    gain_ref, loss_ref, growth_ref, weight_ref, mask_ref = refs[count : count + 5]
    rest = refs[count + 5 :]
    if aliased:
        rest = rest[1:]
    out_ref, state, square = rest
    bins = fields[0].shape[1]
    step = pl.program_id(0)
    energy = [jnp.zeros((TILE, LANES), jnp.float32) for _ in range(PAIR)]
    for n in range(count):
        place = pl.multiple_of(where_ref[n] * bins, 16)
        for row in range(PAIR):
            value = fields[n][row]
            state[pl.ds(place, bins), pl.ds(row * LANES, LANES)] = value.astype(jnp.bfloat16)
            square[pl.ds(place, bins), pl.ds(row * LANES, LANES)] = (value * value).astype(jnp.bfloat16)
            weighted = weight_ref[pl.ds(place, bins), :] * value
            energy[row] = energy[row] + jnp.sum(weighted.reshape(bins // TILE, TILE, LANES), axis=0)
    gain = jnp.dot(gain_ref[...], state[...], preferred_element_type=jnp.float32)
    loss = jnp.dot(loss_ref[...], square[...], preferred_element_type=jnp.float32)
    out = out_ref.reshape(bins * TILE, LANES)
    for row in range(PAIR):
        at = step * PAIR + row
        total = jnp.sum(energy[row], axis=0, keepdims=True)
        sea = mask_ref[pl.ds(at, 1), :].astype(jnp.float32)
        scale = sea / (1.0 + 0.5 * total)
        value = fields[0][row]
        grown = growth_ref[...] * value
        part = slice(row * LANES, (row + 1) * LANES)
        fresh = (value + 0.25 * (grown + value * gain[:, part] - loss[:, part])) * scale
        out[pl.ds(at, bins, stride=TILE), :] = fresh


def add_sources(where, fields, kernels, growth, weight, land_mask, block, out, shape):
    count = len(fields)
    bins, _, columns = shape
    every = weight.shape[0]
    cells = pl.BlockSpec((PAIR, bins, columns), lambda i, w: (i, 0, 0))
    table = pl.BlockSpec((bins, every), lambda i, w: (w[0], 0))
    specs = [cells] * count + [
        table,
        table,
        pl.BlockSpec((bins, columns), lambda i, w: (0, 0)),
        pl.BlockSpec((every, columns), lambda i, w: (0, 0)),
        pl.BlockSpec((TILE, columns), lambda i, w: (block, 0)),
    ]
    args = [*fields, *kernels, growth, weight, land_mask]
    aliases = {}
    if out is not None:
        specs.append(pl.BlockSpec(memory_space=pl.ANY))
        args.append(out)
        aliases = {len(args): 0}
    return pl.pallas_call(
        functools.partial(source_kernel, count, out is not None),
        grid_spec=pltpu.PrefetchScalarGridSpec(
            num_scalar_prefetch=1,
            grid=(TILE // PAIR,),
            in_specs=specs,
            out_specs=pl.BlockSpec((bins, TILE, columns), lambda i, w: (0, block, 0)),
            scratch_shapes=[
                pltpu.VMEM((every, PAIR * columns), jnp.bfloat16),
                pltpu.VMEM((every, PAIR * columns), jnp.bfloat16),
            ],
        ),
        out_shape=jax.ShapeDtypeStruct(shape, jnp.float32),
        input_output_aliases=aliases,
        name="sources",
    )(where, *args)


def local(spectra, land_mask, growth, band_weight, kernel_gain, kernel_loss):
    bins, rows, columns = spectra.shape
    every = band_weight.shape[0]
    me = lax.axis_index("bins")
    group = lax.axis_size("bins")
    slabs = lax.axis_size("space")
    chips = group // 2
    speed_x, speed_y = courants(me * bins, bins)
    cx = jnp.broadcast_to(speed_x[:, None], (bins, columns))
    cy = jnp.broadcast_to(speed_y[:, None], (bins, columns))
    mine = lax.dynamic_slice_in_dim(growth, me * bins, bins)
    growth_wide = jnp.broadcast_to(mine[:, None], (bins, columns))
    weight_wide = jnp.broadcast_to(band_weight[:, None], (every, columns))

    partner = [(i, i ^ 1) for i in range(group)]
    shifts = [[(i, (i + 2 * s) % group) for i in range(group)] for s in range(1, chips)]
    came = [(me + group - 2 * s) % group for s in range(1, chips)]
    where = [me, me ^ 1]
    for source in came:
        where += [source, source ^ 1]
    where = jnp.stack(where).astype(jnp.int32)

    blocks = rows // TILE
    order = sequence(rows)
    count = len(order)
    fields = [None] * count
    far = [None] * count
    near = [None] * count
    before = after = None
    for i, block in enumerate(order):
        if i == 1:
            head, tail = edges(spectra, land_mask)
            before = lax.ppermute(tail, "space", [(n, n + 1) for n in range(slabs - 1)])
            after = lax.ppermute(head, "space", [(n + 1, n) for n in range(slabs - 1)])
        halo = before if block == 0 else after if block == blocks - 1 else None
        fields[i] = propagate(spectra, land_mask, cx, cy, block, halo)
        far[i] = [lax.ppermute(fields[i], "bins", s) for s in shifts]
        near[i] = lax.ppermute(fields[i], "bins", partner)

    out = None
    kernels = (kernel_gain, kernel_loss)
    for i, block in enumerate(order):
        parts = [fields[i], near[i]]
        for came_in in far[i]:
            parts += [came_in, lax.ppermute(came_in, "bins", partner)]
        out = add_sources(where, parts, kernels, growth_wide, weight_wide, land_mask, block, out, spectra.shape)
    return out


def sequence(rows):
    blocks = rows // TILE
    return list(range(1, blocks - 1)) + [0, blocks - 1]


def solution(mesh):
    in_specs = (P("bins", "space", None), P("space", None), P(), P(), P(), P())
    out_specs = P("bins", "space", None)
    return jax.shard_map(local, mesh=mesh, in_specs=in_specs, out_specs=out_specs, check_vma=False)
```

```python
import functools
import math

import jax
import jax.numpy as jnp
import numpy as np
from jax import lax
from jax.experimental import pallas as pl
from jax.experimental.pallas import tpu as pltpu
from jax.sharding import PartitionSpec as P


NF = 32
ND = 36
SUBSTEPS = 4
TILE = 8
LANES = 128


def courants(first, count):
    index = first + jnp.arange(count, dtype=jnp.int32)
    freq = (index // ND).astype(jnp.float32)
    direc = (index % ND).astype(jnp.float32)
    group = 1.0 / (1.0 + 2.3 * freq / max(NF - 1, 1))
    theta = 2.0 * math.pi * (direc + 0.5) / ND
    return (0.9 * group * jnp.cos(theta), 0.9 * group * jnp.sin(theta))


def edge_kernel(low_ref, high_ref, low_mask, high_mask, head_ref, tail_ref):
    bins = low_ref.shape[0]
    low = low_ref.reshape(bins * TILE, LANES)
    high = high_ref.reshape(bins * TILE, LANES)
    for row in range(SUBSTEPS):
        behind = TILE - SUBSTEPS + row
        head_ref[row, pl.ds(0, bins), :] = low[pl.ds(row, bins, stride=TILE), :]
        tail_ref[row, pl.ds(0, bins), :] = high[pl.ds(behind, bins, stride=TILE), :]
        sea_low = low_mask[pl.ds(row, 1), :].astype(jnp.float32)
        sea_high = high_mask[pl.ds(behind, 1), :].astype(jnp.float32)
        head_ref[row, pl.ds(bins, TILE), :] = jnp.broadcast_to(sea_low, (TILE, LANES))
        tail_ref[row, pl.ds(bins, TILE), :] = jnp.broadcast_to(sea_high, (TILE, LANES))


def edges(spectra, land_mask):
    bins, rows, columns = spectra.shape
    last = rows // TILE - 1
    shape = jax.ShapeDtypeStruct((SUBSTEPS, bins + TILE, columns), jnp.float32)
    whole = pl.BlockSpec((SUBSTEPS, bins + TILE, columns), lambda i: (0, 0, 0))
    return pl.pallas_call(
        edge_kernel,
        grid=(1,),
        in_specs=[
            pl.BlockSpec((bins, TILE, columns), lambda i: (0, 0, 0)),
            pl.BlockSpec((bins, TILE, columns), lambda i: (0, last, 0)),
            pl.BlockSpec((TILE, columns), lambda i: (0, 0)),
            pl.BlockSpec((TILE, columns), lambda i: (last, 0)),
        ],
        out_specs=[whole, whole],
        out_shape=[shape, shape],
        name="edges",
    )(spectra, spectra, land_mask, land_mask)


def fill_sea(first, last, prev_mask, mid_mask, next_mask, halo_mask, sea_scr):
    for k in range(TILE + 2 * SUBSTEPS):
        if k < SUBSTEPS:
            if first:
                row = halo_mask[k, pl.ds(0, 1), :]
            else:
                row = prev_mask[pl.ds(TILE - SUBSTEPS + k, 1), :].astype(jnp.float32)
        elif k < SUBSTEPS + TILE:
            row = mid_mask[pl.ds(k - SUBSTEPS, 1), :].astype(jnp.float32)
        elif last:
            row = halo_mask[k - SUBSTEPS - TILE, pl.ds(0, 1), :]
        else:
            row = next_mask[pl.ds(k - SUBSTEPS - TILE, 1), :].astype(jnp.float32)
        sea_scr[k] = jnp.broadcast_to(row, (TILE, LANES))


def general_body(first, last, prev_ref, mid_ref, next_ref, halo_ref, cx_ref, cy_ref, sea_scr, target):
    bins = mid_ref.shape[0]
    window = TILE + 2 * SUBSTEPS
    mid = mid_ref.reshape(bins * TILE, LANES)
    before = None if first else prev_ref.reshape(bins * TILE, LANES)
    after = None if last else next_ref.reshape(bins * TILE, LANES)
    lane = lax.broadcasted_iota(jnp.int32, (TILE, LANES), 1)

    def body(tile, carry):
        base = pl.multiple_of(tile * TILE, TILE)
        origin = tile * (TILE * TILE)
        cx = cx_ref[pl.ds(base, TILE), :]
        cy = cy_ref[pl.ds(base, TILE), :]
        ax = jnp.abs(cx)
        ay = jnp.abs(cy)
        east = cx > 0.0
        from_left = (cy > 0.0) & (lane > 0)
        from_right = (cy <= 0.0) & (lane < LANES - 1)

        def load(k):
            if k < SUBSTEPS:
                if first:
                    return halo_ref[k, pl.ds(base, TILE), :]
                return before[pl.ds(origin + TILE - SUBSTEPS + k, TILE, stride=TILE), :]
            if k < SUBSTEPS + TILE:
                return mid[pl.ds(origin + k - SUBSTEPS, TILE, stride=TILE), :]
            if last:
                return halo_ref[k - SUBSTEPS - TILE, pl.ds(base, TILE), :]
            return after[pl.ds(origin + k - SUBSTEPS - TILE, TILE, stride=TILE), :]

        field = [load(k) for k in range(window)]
        for step in range(SUBSTEPS):
            start = step + 1
            fresh = []
            for k in range(start, window - start):
                here = k - step
                value = field[here]
                source = jnp.where(east, field[here - 1], field[here + 1])
                value = value - ax * (value - source)
                left = pltpu.roll(value, 1, 1)
                right = pltpu.roll(value, LANES - 1, 1)
                source = jnp.where(from_left, left, jnp.where(from_right, right, 0.0))
                value = value - ay * (value - source)
                fresh.append(sea_scr[k] * value)
            field = fresh
        for row in range(TILE):
            target[row, pl.ds(base, TILE), :] = field[row]
        return carry

    lax.fori_loop(0, bins // TILE, body, 0)


def quadrant_body(quadrant, first, last, mid_ref, outer_ref, halo_ref, unit_ref, me_ref, sea_scr, target, turns):
    octet, quarter = mid_ref.shape[:2]
    flat = octet * quarter * TILE
    mid = mid_ref.reshape(flat, LANES)
    outer = outer_ref.reshape(flat, LANES)
    lane = lax.broadcasted_iota(jnp.int32, (TILE, LANES), 1)
    east = quadrant in (0, 3)
    north = quadrant in (0, 1)
    edge = lane == (0 if north else LANES - 1)
    beyond = first if east else last
    skip = TILE - SUBSTEPS if east else 0
    octave = me_ref[0] * octet + lax.broadcasted_iota(jnp.int32, (TILE, LANES), 0)
    speed = 0.9 * (1.0 / (1.0 + 2.3 * octave.astype(jnp.float32) / max(NF - 1, 1)))

    def body(turn, carry):
        direction = quadrant * quarter + turn
        comb = pl.ds(direction, TILE, stride=ND)

        def cells(ref, row):
            return ref[pl.ds(turn * TILE + row, TILE, stride=quarter * TILE), :]

        ax = speed * unit_ref[0, direction]
        ay = speed * unit_ref[1, direction]
        stay = 1.0 - ax
        keep = 1.0 - ay
        take = jnp.where(edge, 0.0, ay)
        inner = [cells(mid, row) for row in range(TILE)]
        if beyond:
            upwind = [halo_ref[row, comb, :] for row in range(SUBSTEPS)]
        else:
            upwind = [cells(outer, skip + row) for row in range(SUBSTEPS)]
        field = upwind + inner if east else inner + upwind
        for step in range(SUBSTEPS):
            fresh = []
            for k in range(len(field) - 1):
                if east:
                    value, source, at = field[k + 1], field[k], step + 1 + k
                else:
                    value, source, at = field[k], field[k + 1], SUBSTEPS + k
                value = stay * value + ax * source
                aside = pltpu.roll(value, 1 if north else LANES - 1, 1)
                fresh.append(sea_scr[at] * (keep * value + take * aside))
            field = fresh
        for row in range(TILE):
            target[row, comb, :] = field[row]
        return carry

    lax.fori_loop(0, quarter, body, 0, unroll=turns)


def by_quadrant(bins):
    return bins == TILE * ND and ND % 4 == 0


def advance(first, last, cells, halo_ref, masks, halo_mask, speeds, sea_scr, target, turns=ND // 4):
    part = pl.program_id(1)

    @pl.when(part == 0)
    def _():
        fill_sea(first, last, *masks, halo_mask, sea_scr)

    if len(cells) == 3:
        general_body(first, last, *cells, halo_ref, *speeds, sea_scr, target)
        return
    for quadrant in range(4):

        @pl.when(part == quadrant)
        def _(quadrant=quadrant):
            quadrant_body(quadrant, first, last, *cells, halo_ref, *speeds, sea_scr, target, turns)


def cell_inputs(spectra, land_mask, at):
    bins, rows, columns = spectra.shape
    last_block = rows // TILE - 1

    def near(shift):
        return lambda i, *p: jnp.clip(at(i, *p) + shift, 0, last_block)

    if by_quadrant(bins):
        whole = spectra.reshape(TILE, ND, rows, columns)
        shape = (TILE, ND // 4, TILE, columns)

        def upwind(i, q, *p):
            shift = jnp.where((q == 0) | (q == 3), -1, 1)
            return (0, q, jnp.clip(at(i, *p) + shift, 0, last_block), 0)

        specs = [pl.BlockSpec(shape, lambda i, q, *p: (0, q, at(i, *p), 0)), pl.BlockSpec(shape, upwind)]
        args = [whole] * 2
        parts = 4
    else:
        shape = (bins, TILE, columns)
        specs = [pl.BlockSpec(shape, lambda i, q, *p, f=near(k): (0, f(i, *p), 0)) for k in (-1, 0, 1)]
        args = [spectra] * 3
        parts = 1
    specs += [pl.BlockSpec((TILE, columns), lambda i, q, *p, f=near(k): (f(i, *p), 0)) for k in (-1, 0, 1)]
    return specs, args + [land_mask] * 3, parts


def speed_inputs(bins, columns, me):
    if by_quadrant(bins):
        theta = 2.0 * np.pi * (np.arange(ND) + 0.5) / ND
        units = np.abs(np.stack([np.cos(theta), np.sin(theta)])).astype(np.float32)
        specs = [pl.BlockSpec(memory_space=pltpu.SMEM)] * 2
        return specs, [jnp.asarray(units), me.reshape(1)]
    speeds = courants(me * bins, bins)
    specs = [pl.BlockSpec((bins, columns), lambda *_: (0, 0))] * 2
    return specs, [jnp.broadcast_to(c[:, None], (bins, columns)) for c in speeds]


def propagate_kernel(first, last, cells, turns, _, *refs):
    fields, masks, rest = refs[:cells], refs[cells : cells + 3], refs[cells + 3 :]
    halo_ref = halo_mask = None
    if first or last:
        halo_ref, halo_mask, rest = rest[0], rest[1], rest[2:]
    *speeds, out_ref, sea_scr = rest
    advance(first, last, fields, halo_ref, masks, halo_mask, speeds, sea_scr, out_ref, turns)


def propagate(spectra, land_mask, speeds, block, halo=None, first=False, turns=ND // 4):
    bins, _, columns = spectra.shape
    last = halo is not None and not first
    specs, args, parts = cell_inputs(spectra, land_mask, lambda i, p: p[0])
    cells = len(args) - 3
    if first or last:
        specs.append(pl.BlockSpec((SUBSTEPS, bins, columns), lambda *_: (0, 0, 0)))
        specs.append(pl.BlockSpec((SUBSTEPS, TILE, columns), lambda *_: (0, bins // TILE, 0)))
        args += [halo, halo]
    return pl.pallas_call(
        functools.partial(propagate_kernel, first, last, cells, turns),
        grid_spec=pltpu.PrefetchScalarGridSpec(
            num_scalar_prefetch=1,
            grid=(1, parts),
            in_specs=specs + speeds[0],
            out_specs=pl.BlockSpec((TILE, bins, columns), lambda *_: (0, 0, 0)),
            scratch_shapes=[pltpu.VMEM((TILE + 2 * SUBSTEPS, TILE, columns), jnp.float32)],
        ),
        out_shape=jax.ShapeDtypeStruct((TILE, bins, columns), jnp.float32),
        name="propagate",
    )(jnp.full((1,), block, jnp.int32), *args, *speeds[1])


PAIR = 2


def source_kernel(count, aliased, where_ref, _, *refs):
    fields = refs[:count]
    gain_ref, loss_ref, growth_ref, weight_ref, mask_ref = refs[count : count + 5]
    rest = refs[count + 5 :]
    if aliased:
        rest = rest[1:]
    out_ref, state, square = rest
    bins = fields[0].shape[1]
    step = pl.program_id(0)
    energy = [jnp.zeros((TILE, LANES), jnp.float32) for _ in range(PAIR)]
    for n in range(count):
        place = pl.multiple_of(where_ref[n] * bins, 16)
        for row in range(PAIR):
            value = fields[n][row]
            state[pl.ds(place, bins), pl.ds(row * LANES, LANES)] = value.astype(jnp.bfloat16)
            square[pl.ds(place, bins), pl.ds(row * LANES, LANES)] = (value * value).astype(jnp.bfloat16)
            weighted = weight_ref[pl.ds(place, bins), :] * value
            energy[row] = energy[row] + jnp.sum(weighted.reshape(bins // TILE, TILE, LANES), axis=0)
    gain = jnp.dot(gain_ref[...], state[...], preferred_element_type=jnp.float32)
    loss = jnp.dot(loss_ref[...], square[...], preferred_element_type=jnp.float32)
    out = out_ref.reshape(bins * TILE, LANES)
    for row in range(PAIR):
        at = step * PAIR + row
        total = jnp.sum(energy[row], axis=0, keepdims=True)
        sea = mask_ref[pl.ds(at, 1), :].astype(jnp.float32)
        scale = sea / (1.0 + 0.5 * total)
        value = fields[0][row]
        grown = growth_ref[...] * value
        part = slice(row * LANES, (row + 1) * LANES)
        fresh = (value + 0.25 * (grown + value * gain[:, part] - loss[:, part])) * scale
        out[pl.ds(at, bins, stride=TILE), :] = fresh


def add_sources(where, fields, kernels, growth, weight, land_mask, block, out, shape):
    count = len(fields)
    bins, _, columns = shape
    every = weight.shape[0]
    cells = pl.BlockSpec((PAIR, bins, columns), lambda i, w, b: (i, 0, 0))
    table = pl.BlockSpec((bins, every), lambda i, w, b: (w[0], 0))
    specs = [cells] * count + [
        table,
        table,
        pl.BlockSpec((bins, columns), lambda i, w, b: (0, 0)),
        pl.BlockSpec((every, columns), lambda i, w, b: (0, 0)),
        pl.BlockSpec((TILE, columns), lambda i, w, b: (b[0], 0)),
    ]
    args = [*fields, *kernels, growth, weight, land_mask]
    aliases = {}
    if out is not None:
        specs.append(pl.BlockSpec(memory_space=pl.ANY))
        args.append(out)
        aliases = {len(args) + 1: 0}
    return pl.pallas_call(
        functools.partial(source_kernel, count, out is not None),
        grid_spec=pltpu.PrefetchScalarGridSpec(
            num_scalar_prefetch=2,
            grid=(TILE // PAIR,),
            in_specs=specs,
            out_specs=pl.BlockSpec((bins, TILE, columns), lambda i, w, b: (0, b[0], 0)),
            scratch_shapes=[
                pltpu.VMEM((every, PAIR * columns), jnp.bfloat16),
                pltpu.VMEM((every, PAIR * columns), jnp.bfloat16),
            ],
        ),
        out_shape=jax.ShapeDtypeStruct(shape, jnp.float32),
        input_output_aliases=aliases,
        name="sources",
    )(where, jnp.full((1,), block, jnp.int32), *args)


def plan_kernel(mask_ref, base_ref, order_ref, least_ref, room_ref, spot_ref, group_ref, over_ref):
    sea = mask_ref[...].astype(jnp.float32)
    marks = sea.astype(jnp.bfloat16)
    row = lax.broadcasted_iota(jnp.int32, (LANES, LANES), 0)
    lane = lax.broadcasted_iota(jnp.int32, (LANES, LANES), 1)
    ahead = (row < lane).astype(jnp.float32).astype(jnp.bfloat16)
    every = jnp.ones((LANES, LANES), jnp.bfloat16)
    rank = jnp.dot(marks, ahead, preferred_element_type=jnp.float32)
    count = jnp.dot(marks, every, preferred_element_type=jnp.float32)
    counts = count.astype(jnp.bfloat16)
    start = jnp.dot(base_ref[...], counts, preferred_element_type=jnp.float32)
    start = jnp.maximum(start, least_ref[...])
    start = start + jnp.dot(order_ref[...], counts, preferred_element_type=jnp.float32)
    group = lax.shift_right_logical(start.astype(jnp.int32), 7)
    spot = start.astype(jnp.int32) - group * LANES + rank.astype(jnp.int32)
    spot_ref[...] = jnp.where(sea > 0.0, spot, -1)
    group_ref[...] = group
    excess = jnp.max(start + count - room_ref[...], axis=0, keepdims=True)
    over_ref[...] = jnp.broadcast_to((excess > 0.0).astype(jnp.int32), (TILE, LANES))


def plan(land_mask, chunks):
    rows, columns = land_mask.shape
    base = np.zeros((rows, rows), np.float32)
    order = np.zeros((rows, rows), np.float32)
    least = np.zeros((rows, columns), np.float32)
    room = np.full((rows, columns), 2.0 * rows * columns, np.float32)
    for blocks, packed in chunks:
        if packed is None:
            continue
        for k, block in enumerate(blocks):
            own = np.arange(TILE * block, TILE * block + TILE)
            for earlier in blocks[:k]:
                base[own, TILE * earlier : TILE * earlier + TILE] = 1.0
            for row in own:
                order[row, own[0] : row] = 1.0
            room[own] = LANES * sum(packed)
            if 0 in blocks and block == 0:
                room[own] = LANES * sum(packed[:-1])
            if 0 in blocks and k == len(blocks) - 1:
                least[own] = LANES * sum(packed[:-2])
    table = jax.ShapeDtypeStruct((rows, columns), jnp.int32)
    small = jax.ShapeDtypeStruct((TILE, columns), jnp.int32)
    tables = (jnp.asarray(base, jnp.bfloat16), jnp.asarray(order, jnp.bfloat16), jnp.asarray(least), jnp.asarray(room))
    return pl.pallas_call(plan_kernel, out_shape=[table, table, small], name="plan")(land_mask, *tables)


def listed(blocks):
    def at(i, *_):
        block = blocks[0]
        for k, b in enumerate(blocks[1:], 1):
            block = jnp.where(i == k, b, block)
        return block

    return at


def pack_kernel(edge, blocks, packed, cells, group_ref, *refs):
    fields, masks, refs = refs[:cells], refs[cells : cells + 3], refs[cells + 3 :]
    if edge:
        before, before_mask, after, after_mask = refs[:4]
        refs = refs[4:]
    spot_ref, *speeds = refs[:3]
    outs = refs[3 : 3 + len(packed)]
    field, total, sea_scr = refs[3 + len(packed) :]
    step, part = pl.program_id(0), pl.program_id(1)
    steps, parts = pl.num_programs(0), pl.num_programs(1)
    room = sum(packed)

    @pl.when((step == 0) & (part == 0))
    def _():
        total[...] = jnp.zeros_like(total)

    first = blocks.index(0) if edge else -1
    last = len(blocks) - 1 if edge else -1

    @pl.when((step != first) & (step != last))
    def _():
        advance(False, False, fields, None, masks, None, speeds, sea_scr, field)

    if edge:

        @pl.when(step == first)
        def _():
            advance(True, False, fields, before, masks, before_mask, speeds, sea_scr, field)

        @pl.when(step == last)
        def _():
            advance(False, True, fields, after, masks, after_mask, speeds, sea_scr, field)

    slot = lax.broadcasted_iota(jnp.int32, (2 * LANES, LANES), 0)

    def gather(row, carry):
        at = jnp.minimum(group_ref[listed(blocks)(step) * TILE + row], room)
        spots = spot_ref[pl.ds(row, 1), :]
        pick = jnp.where(slot == spots, 1.0, 0.0).astype(jnp.bfloat16)
        value = field[row]
        high = value.astype(jnp.bfloat16)
        low = (value - high.astype(jnp.float32)).astype(jnp.bfloat16)
        both = jnp.concatenate([high, low], axis=1)
        picks = jnp.concatenate([pick, pick], axis=1)
        moved = lax.dot_general(both, picks, (((1,), (1,)), ((), ())), preferred_element_type=jnp.float32)
        total[at] = total[at] + moved[:, :LANES]
        total[at + 1] = total[at + 1] + moved[:, LANES:]
        return carry

    @pl.when(part == parts - 1)
    def _():
        lax.fori_loop(0, TILE, gather, 0, unroll=TILE)

    @pl.when((step == steps - 1) & (part == parts - 1))
    def _():
        start = 0
        for size, out in zip(packed, outs):
            for k in range(size):
                out[k] = total[start + k]
            start += size


def pack(spectra, land_mask, speeds, blocks, packed, groups, spots, halos):
    bins, _, columns = spectra.shape
    edge = halos is not None
    at = listed(blocks)
    specs, args, parts = cell_inputs(spectra, land_mask, at)
    cells = len(args) - 3
    if edge:
        wide = pl.BlockSpec((SUBSTEPS, bins, columns), lambda i, q, g: (0, 0, 0))
        sea = pl.BlockSpec((SUBSTEPS, TILE, columns), lambda i, q, g: (0, bins // TILE, 0))
        specs += [wide, sea, wide, sea]
        args += [halos[0], halos[0], halos[1], halos[1]]
    specs += [pl.BlockSpec((TILE, columns), lambda i, q, g: (at(i), 0))] + speeds[0]
    return pl.pallas_call(
        functools.partial(pack_kernel, edge, blocks, packed, cells),
        grid_spec=pltpu.PrefetchScalarGridSpec(
            num_scalar_prefetch=1,
            grid=(len(blocks), parts),
            in_specs=specs,
            out_specs=[pl.BlockSpec((n, bins, columns), lambda i, q, g: (0, 0, 0)) for n in packed],
            scratch_shapes=[
                pltpu.VMEM((TILE, bins, columns), jnp.float32),
                pltpu.VMEM((sum(packed) + 2, bins, columns), jnp.float32),
                pltpu.VMEM((TILE + 2 * SUBSTEPS, TILE, columns), jnp.float32),
            ],
        ),
        out_shape=[jax.ShapeDtypeStruct((n, bins, columns), jnp.float32) for n in packed],
        name="pack",
    )(groups, *args, spots, *speeds[1])


def packed_sources_kernel(count, size, where_ref, *refs):
    fields = refs[: PAIR * count]
    gain_ref, loss_ref, growth_ref, weight_ref, out_ref = refs[PAIR * count : PAIR * count + 5]
    state, square, gain, loss = refs[PAIR * count + 5 :]
    bins = fields[0].shape[1]
    step = pl.program_id(0)
    half = 2 * TILE

    energy = tuple(jnp.zeros((TILE, LANES), jnp.float32) for _ in range(PAIR))
    for n in range(count):
        place = pl.multiple_of(where_ref[n] * bins, half)

        def convert(tile, energy, n=n, place=place):
            base = pl.multiple_of(tile * half, half)
            to = pl.ds(pl.multiple_of(place + base, half), half)
            weight = weight_ref[to, :]
            fresh = []
            for k in range(PAIR):
                value = fields[PAIR * n + k][0, pl.ds(base, half), :]
                lanes = pl.ds(k * LANES, LANES)
                state[to, lanes] = value.astype(jnp.bfloat16)
                square[to, lanes] = (value * value).astype(jnp.bfloat16)
                weighted = weight * value
                fresh.append(energy[k] + weighted[:TILE] + weighted[TILE:])
            return tuple(fresh)

        energy = lax.fori_loop(0, bins // half, convert, energy, unroll=bins // half)
    gain[...] = jnp.dot(gain_ref[...], state[...], preferred_element_type=jnp.float32)
    loss[...] = jnp.dot(loss_ref[...], square[...], preferred_element_type=jnp.float32)
    scales = []
    for k in range(PAIR):
        total = jnp.sum(energy[k], axis=0, keepdims=True)
        scales.append(jnp.broadcast_to(1.0 / (1.0 + 0.5 * total), (TILE, LANES)))

    def finish(tile, carry):
        part = pl.ds(pl.multiple_of(tile * TILE, TILE), TILE)
        grow = growth_ref[part, :]
        for k in range(PAIR):
            value = fields[k][0, part, :]
            lanes = pl.ds(k * LANES, LANES)
            change = grow * value + value * gain[part, lanes] - loss[part, lanes]
            to = jnp.minimum(step * PAIR + k, size - 1)
            out_ref[to, part, :] = (value + 0.25 * change) * scales[k]
        return carry

    lax.fori_loop(0, bins // TILE, finish, 0, unroll=bins // TILE)


def packed_sources(where, fields, kernels, growth, weight):
    count = len(fields)
    size, bins, columns = fields[0].shape
    every = weight.shape[0]
    one = [
        pl.BlockSpec((1, bins, columns), lambda i, w, k=k: (jnp.minimum(i * PAIR + k, size - 1), 0, 0))
        for k in range(PAIR)
    ]
    table = pl.BlockSpec((bins, every), lambda i, w: (w[0], 0))
    specs = one * count + [
        table,
        table,
        pl.BlockSpec((bins, columns), lambda i, w: (0, 0)),
        pl.BlockSpec((every, columns), lambda i, w: (0, 0)),
    ]
    args = [f for field in fields for f in [field] * PAIR]
    return pl.pallas_call(
        functools.partial(packed_sources_kernel, count, size),
        grid_spec=pltpu.PrefetchScalarGridSpec(
            num_scalar_prefetch=1,
            grid=((size + PAIR - 1) // PAIR,),
            in_specs=specs,
            out_specs=pl.BlockSpec((size, bins, columns), lambda i, w: (0, 0, 0)),
            scratch_shapes=[
                pltpu.VMEM((every, PAIR * columns), jnp.bfloat16),
                pltpu.VMEM((every, PAIR * columns), jnp.bfloat16),
                pltpu.VMEM((bins, PAIR * columns), jnp.float32),
                pltpu.VMEM((bins, PAIR * columns), jnp.float32),
            ],
        ),
        out_shape=jax.ShapeDtypeStruct((size, bins, columns), jnp.float32),
        name="packed_sources",
    )(where, *args, *kernels, growth, weight)


def spread_kernel(base, packed, skip, group_ref, *refs):
    parts = refs[: len(packed)]
    spot_ref, _, out_ref, both = refs[len(packed) :]
    step = pl.program_id(0)
    bins = parts[0].shape[1]
    room = sum(packed)

    @pl.when(step == 0)
    def _():
        start = 0
        for size, part in zip(packed, parts):

            def split(k, carry, part=part, start=start):
                value = part[k]
                high = value.astype(jnp.bfloat16)
                both[start + k, :, :LANES] = high
                both[start + k, :, LANES:] = (value - high.astype(jnp.float32)).astype(jnp.bfloat16)
                return carry

            lax.fori_loop(0, size, split, 0)
            start += size

    slot = lax.broadcasted_iota(jnp.int32, (LANES, LANES), 0)
    out = out_ref.reshape(bins * TILE, LANES)
    for row in range(TILE):
        at = jnp.clip(group_ref[(base + step) * TILE + row] - skip, 0, room - 1)
        after = jnp.minimum(at + 1, room - 1)
        spots = spot_ref[pl.ds(row, 1), :]
        near = jnp.where(slot == spots, 1.0, 0.0).astype(jnp.bfloat16)
        far = jnp.where(slot + LANES == spots, 1.0, 0.0).astype(jnp.bfloat16)
        value = jnp.dot(both[at], jnp.concatenate([near, near], axis=0), preferred_element_type=jnp.float32)
        value = value + jnp.dot(both[after], jnp.concatenate([far, far], axis=0), preferred_element_type=jnp.float32)
        out[pl.ds(row, bins, stride=TILE), :] = value


def spread(parts, groups, spots, blocks, out, skip=0):
    bins, _, columns = out.shape
    packed = [p.shape[0] for p in parts]
    base = blocks[0]
    at = lambda i: base + i
    specs = [pl.BlockSpec((n, bins, columns), lambda i, g: (0, 0, 0)) for n in packed]
    specs += [pl.BlockSpec((TILE, columns), lambda i, g: (at(i), 0)), pl.BlockSpec(memory_space=pl.ANY)]
    return pl.pallas_call(
        functools.partial(spread_kernel, base, packed, skip),
        grid_spec=pltpu.PrefetchScalarGridSpec(
            num_scalar_prefetch=1,
            grid=(len(blocks),),
            in_specs=specs,
            out_specs=pl.BlockSpec((bins, TILE, columns), lambda i, g: (0, at(i), 0)),
            scratch_shapes=[pltpu.VMEM((sum(packed), bins, 2 * columns), jnp.bfloat16)],
        ),
        out_shape=jax.ShapeDtypeStruct(out.shape, jnp.float32),
        input_output_aliases={len(parts) + 2: 0},
        name="spread",
    )(groups, *parts, spots, out)


def layout(rows):
    last = rows // TILE - 1

    def room(blocks):
        points = len(blocks) * TILE * LANES
        return -(-points * 25 // (32 * LANES))

    inner = list(range(2, last))
    chunks = [([1], None)]
    while len(inner) > 2:
        blocks, inner = inner[:3], inner[3:]
        chunks.append((blocks, cut(room(blocks), 6)))
    edge = inner + [0, last]
    chunks.append((edge, cut(room(edge) - 12, 6) + [4, 4, 4]))
    return chunks


def cut(groups, size):
    pieces = max(groups // size, 1)
    return [groups // pieces + (k < groups % pieces) for k in range(pieces)]


def local(spectra, land_mask, growth, band_weight, kernel_gain, kernel_loss):
    bins, rows, columns = spectra.shape
    every = band_weight.shape[0]
    me = lax.axis_index("bins")
    group = lax.axis_size("bins")
    slabs = lax.axis_size("space")
    chips = group // 2
    last = rows // TILE - 1
    kernels = (kernel_gain, kernel_loss)
    partner = [(i, i ^ 1) for i in range(group)]
    shifts = [[(i, (i + 2 * s) % group) for i in range(group)] for s in range(1, chips)]
    chunks = layout(rows)

    speeds = speed_inputs(bins, columns, me)
    mine = lax.dynamic_slice_in_dim(growth, me * bins, bins)
    growth_wide = jnp.broadcast_to(mine[:, None], (bins, columns))
    weight_wide = jnp.broadcast_to(band_weight[:, None], (every, columns))
    came = [(me + group - 2 * s) % group for s in range(1, chips)]
    where = [me, me ^ 1]
    for source in came:
        where += [source, source ^ 1]
    where = jnp.stack(where).astype(jnp.int32)

    def exchange(piece):
        far = [lax.ppermute(piece, "bins", s) for s in shifts]
        near = lax.ppermute(piece, "bins", partner)
        parts = [piece, near]
        for came_in in far:
            parts += [came_in, lax.ppermute(came_in, "bins", partner)]
        return parts

    whole = propagate(spectra, land_mask, speeds, 1)
    gathered = [[exchange(whole)]]
    spots, group_rows, over = plan(land_mask, chunks)
    groups = group_rows[:, 0]
    head, tail = edges(spectra, land_mask)
    before = lax.ppermute(tail, "space", [(n, n + 1) for n in range(slabs - 1)])
    after = lax.ppermute(head, "space", [(n + 1, n) for n in range(slabs - 1)])
    reach = 1
    while reach < slabs:
        ring = [(n, (n + reach) % slabs) for n in range(slabs)]
        over = jnp.maximum(over, lax.ppermute(over, "space", ring))
        reach *= 2

    for c, (blocks, packed) in enumerate(chunks[1:], 1):
        halos = (before, after) if 0 in blocks else None
        pieces = pack(spectra, land_mask, speeds, blocks, packed, groups, spots, halos)
        gathered.append([])
        for piece in pieces:
            gathered[c].append(exchange(piece))

    out = add_sources(where, gathered[0][0], kernels, growth_wide, weight_wide, land_mask, 1, None, spectra.shape)
    for c, (blocks, packed) in enumerate(chunks[1:], 1):
        parts = []
        for fields in gathered[c]:
            parts.append(packed_sources(where, fields, kernels, growth_wide, weight_wide))
            if 0 in blocks and len(parts) == len(packed) - 2:
                out = spread(parts, groups, spots, blocks[:-2], out)
            if 0 in blocks and len(parts) == len(packed) - 1:
                crowded, parts[-1] = lax.optimization_barrier((over[0, 0] > 0, parts[-1]))
                out = spread(parts, groups, spots, [0], out)
        if 0 in blocks:
            out = spread(parts[-2:], groups, spots, [last], out, sum(packed[:-2]))
        else:
            out = spread(parts, groups, spots, blocks, out)

    def again(out):
        def redo(block, out, halo=None, first=False):
            field = propagate(spectra, land_mask, speeds, block, halo, first, 1)
            fields = [field, lax.ppermute(field, "bins", partner)]
            for s in shifts:
                came_in = lax.ppermute(field, "bins", s)
                fields += [came_in, lax.ppermute(came_in, "bins", partner)]
            return add_sources(
                where, fields, kernels, growth_wide, weight_wide, land_mask, block, out, spectra.shape
            )

        out = lax.fori_loop(2, last, redo, out)
        return redo(last, redo(0, out, before, True), after)

    return lax.cond(crowded, again, lambda out: out, out)


def solution(mesh):
    in_specs = (P("bins", "space", None), P("space", None), P(), P(), P(), P())
    out_specs = P("bins", "space", None)
    return jax.shard_map(local, mesh=mesh, in_specs=in_specs, out_specs=out_specs, check_vma=False)
```

```python
import functools
import math

import jax
import jax.numpy as jnp
import numpy as np
from jax import lax
from jax.experimental import pallas as pl
from jax.experimental.pallas import tpu as pltpu
from jax.sharding import PartitionSpec as P


NF = 32
ND = 36
SUBSTEPS = 4
TILE = 8
LANES = 128


def courants(first, count):
    index = first + jnp.arange(count, dtype=jnp.int32)
    freq = (index // ND).astype(jnp.float32)
    direc = (index % ND).astype(jnp.float32)
    group = 1.0 / (1.0 + 2.3 * freq / max(NF - 1, 1))
    theta = 2.0 * math.pi * (direc + 0.5) / ND
    return (0.9 * group * jnp.cos(theta), 0.9 * group * jnp.sin(theta))


def edge_kernel(low_ref, high_ref, low_mask, high_mask, head_ref, tail_ref):
    bins = low_ref.shape[0]
    low = low_ref.reshape(bins * TILE, LANES)
    high = high_ref.reshape(bins * TILE, LANES)
    for row in range(SUBSTEPS):
        behind = TILE - SUBSTEPS + row
        head_ref[row, pl.ds(0, bins), :] = low[pl.ds(row, bins, stride=TILE), :]
        tail_ref[row, pl.ds(0, bins), :] = high[pl.ds(behind, bins, stride=TILE), :]
        sea_low = low_mask[pl.ds(row, 1), :].astype(jnp.float32)
        sea_high = high_mask[pl.ds(behind, 1), :].astype(jnp.float32)
        head_ref[row, pl.ds(bins, TILE), :] = jnp.broadcast_to(sea_low, (TILE, LANES))
        tail_ref[row, pl.ds(bins, TILE), :] = jnp.broadcast_to(sea_high, (TILE, LANES))


def edges(spectra, land_mask):
    bins, rows, columns = spectra.shape
    last = rows // TILE - 1
    shape = jax.ShapeDtypeStruct((SUBSTEPS, bins + TILE, columns), jnp.float32)
    whole = pl.BlockSpec((SUBSTEPS, bins + TILE, columns), lambda i: (0, 0, 0))
    return pl.pallas_call(
        edge_kernel,
        grid=(1,),
        in_specs=[
            pl.BlockSpec((bins, TILE, columns), lambda i: (0, 0, 0)),
            pl.BlockSpec((bins, TILE, columns), lambda i: (0, last, 0)),
            pl.BlockSpec((TILE, columns), lambda i: (0, 0)),
            pl.BlockSpec((TILE, columns), lambda i: (last, 0)),
        ],
        out_specs=[whole, whole],
        out_shape=[shape, shape],
        name="edges",
    )(spectra, spectra, land_mask, land_mask)


def fill_sea(first, last, prev_mask, mid_mask, next_mask, halo_mask, sea_scr):
    for k in range(TILE + 2 * SUBSTEPS):
        if k < SUBSTEPS:
            if first:
                row = halo_mask[k, pl.ds(0, 1), :]
            else:
                row = prev_mask[pl.ds(TILE - SUBSTEPS + k, 1), :].astype(jnp.float32)
        elif k < SUBSTEPS + TILE:
            row = mid_mask[pl.ds(k - SUBSTEPS, 1), :].astype(jnp.float32)
        elif last:
            row = halo_mask[k - SUBSTEPS - TILE, pl.ds(0, 1), :]
        else:
            row = next_mask[pl.ds(k - SUBSTEPS - TILE, 1), :].astype(jnp.float32)
        sea_scr[k] = jnp.broadcast_to(row, (TILE, LANES))


def general_body(first, last, prev_ref, mid_ref, next_ref, halo_ref, cx_ref, cy_ref, sea_scr, target):
    bins = mid_ref.shape[0]
    window = TILE + 2 * SUBSTEPS
    mid = mid_ref.reshape(bins * TILE, LANES)
    before = None if first else prev_ref.reshape(bins * TILE, LANES)
    after = None if last else next_ref.reshape(bins * TILE, LANES)
    lane = lax.broadcasted_iota(jnp.int32, (TILE, LANES), 1)

    def body(tile, carry):
        base = pl.multiple_of(tile * TILE, TILE)
        origin = tile * (TILE * TILE)
        cx = cx_ref[pl.ds(base, TILE), :]
        cy = cy_ref[pl.ds(base, TILE), :]
        ax = jnp.abs(cx)
        ay = jnp.abs(cy)
        east = cx > 0.0
        from_left = (cy > 0.0) & (lane > 0)
        from_right = (cy <= 0.0) & (lane < LANES - 1)

        def load(k):
            if k < SUBSTEPS:
                if first:
                    return halo_ref[k, pl.ds(base, TILE), :]
                return before[pl.ds(origin + TILE - SUBSTEPS + k, TILE, stride=TILE), :]
            if k < SUBSTEPS + TILE:
                return mid[pl.ds(origin + k - SUBSTEPS, TILE, stride=TILE), :]
            if last:
                return halo_ref[k - SUBSTEPS - TILE, pl.ds(base, TILE), :]
            return after[pl.ds(origin + k - SUBSTEPS - TILE, TILE, stride=TILE), :]

        field = [load(k) for k in range(window)]
        for step in range(SUBSTEPS):
            start = step + 1
            fresh = []
            for k in range(start, window - start):
                here = k - step
                value = field[here]
                source = jnp.where(east, field[here - 1], field[here + 1])
                value = value - ax * (value - source)
                left = pltpu.roll(value, 1, 1)
                right = pltpu.roll(value, LANES - 1, 1)
                source = jnp.where(from_left, left, jnp.where(from_right, right, 0.0))
                value = value - ay * (value - source)
                fresh.append(sea_scr[k] * value)
            field = fresh
        for row in range(TILE):
            target[row, pl.ds(base, TILE), :] = field[row]
        return carry

    lax.fori_loop(0, bins // TILE, body, 0)


def quadrant_body(quadrant, first, last, mid_ref, outer_ref, halo_ref, unit_ref, me_ref, sea_scr, target, turns):
    octet, quarter = mid_ref.shape[:2]
    flat = octet * quarter * TILE
    mid = mid_ref.reshape(flat, LANES)
    outer = outer_ref.reshape(flat, LANES)
    lane = lax.broadcasted_iota(jnp.int32, (TILE, LANES), 1)
    east = quadrant in (0, 3)
    north = quadrant in (0, 1)
    edge = lane == (0 if north else LANES - 1)
    beyond = first if east else last
    skip = TILE - SUBSTEPS if east else 0
    octave = me_ref[0] * octet + lax.broadcasted_iota(jnp.int32, (TILE, LANES), 0)
    speed = 0.9 * (1.0 / (1.0 + 2.3 * octave.astype(jnp.float32) / max(NF - 1, 1)))

    def body(turn, carry):
        direction = quadrant * quarter + turn
        comb = pl.ds(direction, TILE, stride=ND)

        def cells(ref, row):
            return ref[pl.ds(turn * TILE + row, TILE, stride=quarter * TILE), :]

        ax = speed * unit_ref[0, direction]
        ay = speed * unit_ref[1, direction]
        stay = 1.0 - ax
        keep = 1.0 - ay
        take = jnp.where(edge, 0.0, ay)
        inner = [cells(mid, row) for row in range(TILE)]
        if beyond:
            upwind = [halo_ref[row, comb, :] for row in range(SUBSTEPS)]
        else:
            upwind = [cells(outer, skip + row) for row in range(SUBSTEPS)]
        field = upwind + inner if east else inner + upwind
        for step in range(SUBSTEPS):
            fresh = []
            for k in range(len(field) - 1):
                if east:
                    value, source, at = field[k + 1], field[k], step + 1 + k
                else:
                    value, source, at = field[k], field[k + 1], SUBSTEPS + k
                value = stay * value + ax * source
                aside = pltpu.roll(value, 1 if north else LANES - 1, 1)
                fresh.append(sea_scr[at] * (keep * value + take * aside))
            field = fresh
        for row in range(TILE):
            target[row, comb, :] = field[row]
        return carry

    lax.fori_loop(0, quarter, body, 0, unroll=turns)


def by_quadrant(bins):
    return bins == TILE * ND and ND % 4 == 0


def advance(first, last, cells, halo_ref, masks, halo_mask, speeds, sea_scr, target, turns=ND // 4):
    part = pl.program_id(1)

    @pl.when(part == 0)
    def _():
        fill_sea(first, last, *masks, halo_mask, sea_scr)

    if len(cells) == 3:
        general_body(first, last, *cells, halo_ref, *speeds, sea_scr, target)
        return
    for quadrant in range(4):

        @pl.when(part == quadrant)
        def _(quadrant=quadrant):
            quadrant_body(quadrant, first, last, *cells, halo_ref, *speeds, sea_scr, target, turns)


def cell_inputs(spectra, land_mask, at):
    bins, rows, columns = spectra.shape
    last_block = rows // TILE - 1

    def near(shift):
        return lambda i, *p: jnp.clip(at(i, *p) + shift, 0, last_block)

    if by_quadrant(bins):
        whole = spectra.reshape(TILE, ND, rows, columns)
        shape = (TILE, ND // 4, TILE, columns)

        def upwind(i, q, *p):
            shift = jnp.where((q == 0) | (q == 3), -1, 1)
            return (0, q, jnp.clip(at(i, *p) + shift, 0, last_block), 0)

        specs = [pl.BlockSpec(shape, lambda i, q, *p: (0, q, at(i, *p), 0)), pl.BlockSpec(shape, upwind)]
        args = [whole] * 2
        parts = 4
    else:
        shape = (bins, TILE, columns)
        specs = [pl.BlockSpec(shape, lambda i, q, *p, f=near(k): (0, f(i, *p), 0)) for k in (-1, 0, 1)]
        args = [spectra] * 3
        parts = 1
    specs += [pl.BlockSpec((TILE, columns), lambda i, q, *p, f=near(k): (f(i, *p), 0)) for k in (-1, 0, 1)]
    return specs, args + [land_mask] * 3, parts


def speed_inputs(bins, columns, me):
    if by_quadrant(bins):
        theta = 2.0 * np.pi * (np.arange(ND) + 0.5) / ND
        units = np.abs(np.stack([np.cos(theta), np.sin(theta)])).astype(np.float32)
        specs = [pl.BlockSpec(memory_space=pltpu.SMEM)] * 2
        return specs, [jnp.asarray(units), me.reshape(1)]
    speeds = courants(me * bins, bins)
    specs = [pl.BlockSpec((bins, columns), lambda *_: (0, 0))] * 2
    return specs, [jnp.broadcast_to(c[:, None], (bins, columns)) for c in speeds]


def propagate_kernel(first, last, cells, turns, _, *refs):
    fields, masks, rest = refs[:cells], refs[cells : cells + 3], refs[cells + 3 :]
    halo_ref = halo_mask = None
    if first or last:
        halo_ref, halo_mask, rest = rest[0], rest[1], rest[2:]
    *speeds, out_ref, sea_scr = rest
    advance(first, last, fields, halo_ref, masks, halo_mask, speeds, sea_scr, out_ref, turns)


def propagate(spectra, land_mask, speeds, block, halo=None, first=False, turns=ND // 4):
    bins, _, columns = spectra.shape
    last = halo is not None and not first
    specs, args, parts = cell_inputs(spectra, land_mask, lambda i, p: p[0])
    cells = len(args) - 3
    if first or last:
        specs.append(pl.BlockSpec((SUBSTEPS, bins, columns), lambda *_: (0, 0, 0)))
        specs.append(pl.BlockSpec((SUBSTEPS, TILE, columns), lambda *_: (0, bins // TILE, 0)))
        args += [halo, halo]
    return pl.pallas_call(
        functools.partial(propagate_kernel, first, last, cells, turns),
        grid_spec=pltpu.PrefetchScalarGridSpec(
            num_scalar_prefetch=1,
            grid=(1, parts),
            in_specs=specs + speeds[0],
            out_specs=pl.BlockSpec((TILE, bins, columns), lambda *_: (0, 0, 0)),
            scratch_shapes=[pltpu.VMEM((TILE + 2 * SUBSTEPS, TILE, columns), jnp.float32)],
        ),
        out_shape=jax.ShapeDtypeStruct((TILE, bins, columns), jnp.float32),
        name="propagate",
    )(jnp.full((1,), block, jnp.int32), *args, *speeds[1])


PAIR = 2


def source_kernel(count, aliased, where_ref, _, *refs):
    fields = refs[:count]
    gain_ref, loss_ref, growth_ref, weight_ref, mask_ref = refs[count : count + 5]
    rest = refs[count + 5 :]
    if aliased:
        rest = rest[1:]
    out_ref, state, square = rest
    bins = fields[0].shape[1]
    step = pl.program_id(0)
    energy = [jnp.zeros((TILE, LANES), jnp.float32) for _ in range(PAIR)]
    for n in range(count):
        place = pl.multiple_of(where_ref[n] * bins, 16)
        for row in range(PAIR):
            value = fields[n][row]
            state[pl.ds(place, bins), pl.ds(row * LANES, LANES)] = value.astype(jnp.bfloat16)
            square[pl.ds(place, bins), pl.ds(row * LANES, LANES)] = (value * value).astype(jnp.bfloat16)
            weighted = weight_ref[pl.ds(place, bins), :] * value
            energy[row] = energy[row] + jnp.sum(weighted.reshape(bins // TILE, TILE, LANES), axis=0)
    gain = jnp.dot(gain_ref[...], state[...], preferred_element_type=jnp.float32)
    loss = jnp.dot(loss_ref[...], square[...], preferred_element_type=jnp.float32)
    out = out_ref.reshape(bins * TILE, LANES)
    for row in range(PAIR):
        at = step * PAIR + row
        total = jnp.sum(energy[row], axis=0, keepdims=True)
        sea = mask_ref[pl.ds(at, 1), :].astype(jnp.float32)
        scale = sea / (1.0 + 0.5 * total)
        value = fields[0][row]
        grown = growth_ref[...] * value
        part = slice(row * LANES, (row + 1) * LANES)
        fresh = (value + 0.25 * (grown + value * gain[:, part] - loss[:, part])) * scale
        out[pl.ds(at, bins, stride=TILE), :] = fresh


def add_sources(where, fields, kernels, growth, weight, land_mask, block, out, shape):
    count = len(fields)
    bins, _, columns = shape
    every = weight.shape[0]
    cells = pl.BlockSpec((PAIR, bins, columns), lambda i, w, b: (i, 0, 0))
    table = pl.BlockSpec((bins, every), lambda i, w, b: (w[0], 0))
    specs = [cells] * count + [
        table,
        table,
        pl.BlockSpec((bins, columns), lambda i, w, b: (0, 0)),
        pl.BlockSpec((every, columns), lambda i, w, b: (0, 0)),
        pl.BlockSpec((TILE, columns), lambda i, w, b: (b[0], 0)),
    ]
    args = [*fields, *kernels, growth, weight, land_mask]
    aliases = {}
    if out is not None:
        specs.append(pl.BlockSpec(memory_space=pl.ANY))
        args.append(out)
        aliases = {len(args) + 1: 0}
    return pl.pallas_call(
        functools.partial(source_kernel, count, out is not None),
        grid_spec=pltpu.PrefetchScalarGridSpec(
            num_scalar_prefetch=2,
            grid=(TILE // PAIR,),
            in_specs=specs,
            out_specs=pl.BlockSpec((bins, TILE, columns), lambda i, w, b: (0, b[0], 0)),
            scratch_shapes=[
                pltpu.VMEM((every, PAIR * columns), jnp.bfloat16),
                pltpu.VMEM((every, PAIR * columns), jnp.bfloat16),
            ],
        ),
        out_shape=jax.ShapeDtypeStruct(shape, jnp.float32),
        input_output_aliases=aliases,
        name="sources",
    )(where, jnp.full((1,), block, jnp.int32), *args)


def plan_kernel(mask_ref, base_ref, order_ref, least_ref, room_ref, spot_ref, group_ref, over_ref):
    sea = mask_ref[...].astype(jnp.float32)
    marks = sea.astype(jnp.bfloat16)
    row = lax.broadcasted_iota(jnp.int32, (LANES, LANES), 0)
    lane = lax.broadcasted_iota(jnp.int32, (LANES, LANES), 1)
    ahead = (row < lane).astype(jnp.float32).astype(jnp.bfloat16)
    every = jnp.ones((LANES, LANES), jnp.bfloat16)
    rank = jnp.dot(marks, ahead, preferred_element_type=jnp.float32)
    count = jnp.dot(marks, every, preferred_element_type=jnp.float32)
    counts = count.astype(jnp.bfloat16)
    start = jnp.dot(base_ref[...], counts, preferred_element_type=jnp.float32)
    start = jnp.maximum(start, least_ref[...])
    start = start + jnp.dot(order_ref[...], counts, preferred_element_type=jnp.float32)
    group = lax.shift_right_logical(start.astype(jnp.int32), 7)
    spot = start.astype(jnp.int32) - group * LANES + rank.astype(jnp.int32)
    spot_ref[...] = jnp.where(sea > 0.0, spot, -1)
    group_ref[...] = group
    excess = jnp.max(start + count - room_ref[...], axis=0, keepdims=True)
    over_ref[...] = jnp.broadcast_to((excess > 0.0).astype(jnp.int32), (TILE, LANES))


def plan(land_mask, chunks):
    rows, columns = land_mask.shape
    base = np.zeros((rows, rows), np.float32)
    order = np.zeros((rows, rows), np.float32)
    least = np.zeros((rows, columns), np.float32)
    room = np.full((rows, columns), 2.0 * rows * columns, np.float32)
    for blocks, packed in chunks:
        if packed is None:
            continue
        for k, block in enumerate(blocks):
            own = np.arange(TILE * block, TILE * block + TILE)
            for earlier in blocks[:k]:
                base[own, TILE * earlier : TILE * earlier + TILE] = 1.0
            for row in own:
                order[row, own[0] : row] = 1.0
            room[own] = LANES * sum(packed)
            if 0 in blocks and block == 0:
                room[own] = LANES * sum(packed[:-1])
            if 0 in blocks and k == len(blocks) - 1:
                least[own] = LANES * sum(packed[:-2])
    table = jax.ShapeDtypeStruct((rows, columns), jnp.int32)
    small = jax.ShapeDtypeStruct((TILE, columns), jnp.int32)
    tables = (jnp.asarray(base, jnp.bfloat16), jnp.asarray(order, jnp.bfloat16), jnp.asarray(least), jnp.asarray(room))
    return pl.pallas_call(plan_kernel, out_shape=[table, table, small], name="plan")(land_mask, *tables)


def ballot_kernel(in_ref, out_ref):
    out_ref[...] = in_ref[...]


def ballot(over):
    return pl.pallas_call(ballot_kernel, out_shape=jax.ShapeDtypeStruct(over.shape, over.dtype), name="ballot")(over)


def listed(blocks):
    def at(i, *_):
        block = blocks[0]
        for k, b in enumerate(blocks[1:], 1):
            block = jnp.where(i == k, b, block)
        return block

    return at


def pack_kernel(edge, blocks, packed, cells, group_ref, *refs):
    fields, masks, refs = refs[:cells], refs[cells : cells + 3], refs[cells + 3 :]
    if edge:
        before, before_mask, after, after_mask = refs[:4]
        refs = refs[4:]
    spot_ref, *speeds = refs[:3]
    outs = refs[3 : 3 + len(packed)]
    field, total, sea_scr = refs[3 + len(packed) :]
    step, part = pl.program_id(0), pl.program_id(1)
    steps, parts = pl.num_programs(0), pl.num_programs(1)
    room = sum(packed)

    @pl.when((step == 0) & (part == 0))
    def _():
        total[...] = jnp.zeros_like(total)

    first = blocks.index(0) if edge else -1
    last = len(blocks) - 1 if edge else -1

    @pl.when((step != first) & (step != last))
    def _():
        advance(False, False, fields, None, masks, None, speeds, sea_scr, field)

    if edge:

        @pl.when(step == first)
        def _():
            advance(True, False, fields, before, masks, before_mask, speeds, sea_scr, field)

        @pl.when(step == last)
        def _():
            advance(False, True, fields, after, masks, after_mask, speeds, sea_scr, field)

    slot = lax.broadcasted_iota(jnp.int32, (2 * LANES, LANES), 0)

    def gather(row, carry):
        at = jnp.minimum(group_ref[listed(blocks)(step) * TILE + row], room)
        spots = spot_ref[pl.ds(row, 1), :]
        pick = jnp.where(slot == spots, 1.0, 0.0).astype(jnp.bfloat16)
        value = field[row]
        high = value.astype(jnp.bfloat16)
        low = (value - high.astype(jnp.float32)).astype(jnp.bfloat16)
        both = jnp.concatenate([high, low], axis=1)
        picks = jnp.concatenate([pick, pick], axis=1)
        moved = lax.dot_general(both, picks, (((1,), (1,)), ((), ())), preferred_element_type=jnp.float32)
        total[at] = total[at] + moved[:, :LANES]
        total[at + 1] = total[at + 1] + moved[:, LANES:]
        return carry

    @pl.when(part == parts - 1)
    def _():
        lax.fori_loop(0, TILE, gather, 0, unroll=TILE)

    @pl.when((step == steps - 1) & (part == parts - 1))
    def _():
        start = 0
        for size, out in zip(packed, outs):
            for k in range(size):
                out[k] = total[start + k]
            start += size


def pack(spectra, land_mask, speeds, blocks, packed, groups, spots, halos):
    bins, _, columns = spectra.shape
    edge = halos is not None
    at = listed(blocks)
    specs, args, parts = cell_inputs(spectra, land_mask, at)
    cells = len(args) - 3
    if edge:
        wide = pl.BlockSpec((SUBSTEPS, bins, columns), lambda i, q, g: (0, 0, 0))
        sea = pl.BlockSpec((SUBSTEPS, TILE, columns), lambda i, q, g: (0, bins // TILE, 0))
        specs += [wide, sea, wide, sea]
        args += [halos[0], halos[0], halos[1], halos[1]]
    specs += [pl.BlockSpec((TILE, columns), lambda i, q, g: (at(i), 0))] + speeds[0]
    return pl.pallas_call(
        functools.partial(pack_kernel, edge, blocks, packed, cells),
        grid_spec=pltpu.PrefetchScalarGridSpec(
            num_scalar_prefetch=1,
            grid=(len(blocks), parts),
            in_specs=specs,
            out_specs=[pl.BlockSpec((n, bins, columns), lambda i, q, g: (0, 0, 0)) for n in packed],
            scratch_shapes=[
                pltpu.VMEM((TILE, bins, columns), jnp.float32),
                pltpu.VMEM((sum(packed) + 2, bins, columns), jnp.float32),
                pltpu.VMEM((TILE + 2 * SUBSTEPS, TILE, columns), jnp.float32),
            ],
        ),
        out_shape=[jax.ShapeDtypeStruct((n, bins, columns), jnp.float32) for n in packed],
        name="pack",
    )(groups, *args, spots, *speeds[1])


def packed_sources_kernel(count, size, where_ref, *refs):
    fields = refs[: PAIR * count]
    gain_ref, loss_ref, growth_ref, weight_ref, out_ref = refs[PAIR * count : PAIR * count + 5]
    state, square, gain, loss = refs[PAIR * count + 5 :]
    bins = fields[0].shape[1]
    step = pl.program_id(0)
    half = 2 * TILE

    energy = tuple(jnp.zeros((TILE, LANES), jnp.float32) for _ in range(PAIR))
    for n in range(count):
        place = pl.multiple_of(where_ref[n] * bins, half)

        def convert(tile, energy, n=n, place=place):
            base = pl.multiple_of(tile * half, half)
            to = pl.ds(pl.multiple_of(place + base, half), half)
            weight = weight_ref[to, :]
            fresh = []
            for k in range(PAIR):
                value = fields[PAIR * n + k][0, pl.ds(base, half), :]
                lanes = pl.ds(k * LANES, LANES)
                state[to, lanes] = value.astype(jnp.bfloat16)
                square[to, lanes] = (value * value).astype(jnp.bfloat16)
                weighted = weight * value
                fresh.append(energy[k] + weighted[:TILE] + weighted[TILE:])
            return tuple(fresh)

        energy = lax.fori_loop(0, bins // half, convert, energy, unroll=bins // half)
    gain[...] = jnp.dot(gain_ref[...], state[...], preferred_element_type=jnp.float32)
    loss[...] = jnp.dot(loss_ref[...], square[...], preferred_element_type=jnp.float32)
    scales = []
    for k in range(PAIR):
        total = jnp.sum(energy[k], axis=0, keepdims=True)
        scales.append(jnp.broadcast_to(1.0 / (1.0 + 0.5 * total), (TILE, LANES)))

    def finish(tile, carry):
        part = pl.ds(pl.multiple_of(tile * TILE, TILE), TILE)
        grow = growth_ref[part, :]
        for k in range(PAIR):
            value = fields[k][0, part, :]
            lanes = pl.ds(k * LANES, LANES)
            change = grow * value + value * gain[part, lanes] - loss[part, lanes]
            to = jnp.minimum(step * PAIR + k, size - 1)
            out_ref[to, part, :] = (value + 0.25 * change) * scales[k]
        return carry

    lax.fori_loop(0, bins // TILE, finish, 0, unroll=bins // TILE)


def packed_sources(where, fields, kernels, growth, weight):
    count = len(fields)
    size, bins, columns = fields[0].shape
    every = weight.shape[0]
    one = [
        pl.BlockSpec((1, bins, columns), lambda i, w, k=k: (jnp.minimum(i * PAIR + k, size - 1), 0, 0))
        for k in range(PAIR)
    ]
    table = pl.BlockSpec((bins, every), lambda i, w: (w[0], 0))
    specs = one * count + [
        table,
        table,
        pl.BlockSpec((bins, columns), lambda i, w: (0, 0)),
        pl.BlockSpec((every, columns), lambda i, w: (0, 0)),
    ]
    args = [f for field in fields for f in [field] * PAIR]
    return pl.pallas_call(
        functools.partial(packed_sources_kernel, count, size),
        grid_spec=pltpu.PrefetchScalarGridSpec(
            num_scalar_prefetch=1,
            grid=((size + PAIR - 1) // PAIR,),
            in_specs=specs,
            out_specs=pl.BlockSpec((size, bins, columns), lambda i, w: (0, 0, 0)),
            scratch_shapes=[
                pltpu.VMEM((every, PAIR * columns), jnp.bfloat16),
                pltpu.VMEM((every, PAIR * columns), jnp.bfloat16),
                pltpu.VMEM((bins, PAIR * columns), jnp.float32),
                pltpu.VMEM((bins, PAIR * columns), jnp.float32),
            ],
        ),
        out_shape=jax.ShapeDtypeStruct((size, bins, columns), jnp.float32),
        name="packed_sources",
    )(where, *args, *kernels, growth, weight)


def spread_kernel(base, packed, skip, group_ref, *refs):
    parts = refs[: len(packed)]
    spot_ref, _, out_ref, both = refs[len(packed) :]
    step = pl.program_id(0)
    bins = parts[0].shape[1]
    room = sum(packed)

    @pl.when(step == 0)
    def _():
        start = 0
        for size, part in zip(packed, parts):

            def split(k, carry, part=part, start=start):
                value = part[k]
                high = value.astype(jnp.bfloat16)
                both[start + k, :, :LANES] = high
                both[start + k, :, LANES:] = (value - high.astype(jnp.float32)).astype(jnp.bfloat16)
                return carry

            lax.fori_loop(0, size, split, 0)
            start += size

    slot = lax.broadcasted_iota(jnp.int32, (LANES, LANES), 0)
    out = out_ref.reshape(bins * TILE, LANES)
    for row in range(TILE):
        at = jnp.clip(group_ref[(base + step) * TILE + row] - skip, 0, room - 1)
        after = jnp.minimum(at + 1, room - 1)
        spots = spot_ref[pl.ds(row, 1), :]
        near = jnp.where(slot == spots, 1.0, 0.0).astype(jnp.bfloat16)
        far = jnp.where(slot + LANES == spots, 1.0, 0.0).astype(jnp.bfloat16)
        value = jnp.dot(both[at], jnp.concatenate([near, near], axis=0), preferred_element_type=jnp.float32)
        value = value + jnp.dot(both[after], jnp.concatenate([far, far], axis=0), preferred_element_type=jnp.float32)
        out[pl.ds(row, bins, stride=TILE), :] = value


def spread(parts, groups, spots, blocks, out, skip=0):
    bins, _, columns = out.shape
    packed = [p.shape[0] for p in parts]
    base = blocks[0]
    at = lambda i: base + i
    specs = [pl.BlockSpec((n, bins, columns), lambda i, g: (0, 0, 0)) for n in packed]
    specs += [pl.BlockSpec((TILE, columns), lambda i, g: (at(i), 0)), pl.BlockSpec(memory_space=pl.ANY)]
    return pl.pallas_call(
        functools.partial(spread_kernel, base, packed, skip),
        grid_spec=pltpu.PrefetchScalarGridSpec(
            num_scalar_prefetch=1,
            grid=(len(blocks),),
            in_specs=specs,
            out_specs=pl.BlockSpec((bins, TILE, columns), lambda i, g: (0, at(i), 0)),
            scratch_shapes=[pltpu.VMEM((sum(packed), bins, 2 * columns), jnp.bfloat16)],
        ),
        out_shape=jax.ShapeDtypeStruct(out.shape, jnp.float32),
        input_output_aliases={len(parts) + 2: 0},
        name="spread",
    )(groups, *parts, spots, out)


def layout(rows):
    last = rows // TILE - 1

    def room(blocks):
        points = len(blocks) * TILE * LANES
        return -(-points * 25 // (32 * LANES))

    inner = list(range(2, last))
    chunks = [([1], None)]
    while len(inner) > 2:
        blocks, inner = inner[:3], inner[3:]
        chunks.append((blocks, cut(room(blocks), 6)))
    edge = inner + [0, last]
    chunks.append((edge, cut(room(edge) - 12, 6) + [4, 4, 4]))
    return chunks


def cut(groups, size):
    pieces = max(groups // size, 1)
    return [groups // pieces + (k < groups % pieces) for k in range(pieces)]


def local(spectra, land_mask, growth, band_weight, kernel_gain, kernel_loss):
    bins, rows, columns = spectra.shape
    every = band_weight.shape[0]
    me = lax.axis_index("bins")
    group = lax.axis_size("bins")
    slabs = lax.axis_size("space")
    chips = group // 2
    last = rows // TILE - 1
    kernels = (kernel_gain, kernel_loss)
    partner = [(i, i ^ 1) for i in range(group)]
    shifts = [[(i, (i + 2 * s) % group) for i in range(group)] for s in range(1, chips)]
    chunks = layout(rows)

    speeds = speed_inputs(bins, columns, me)
    mine = lax.dynamic_slice_in_dim(growth, me * bins, bins)
    growth_wide = jnp.broadcast_to(mine[:, None], (bins, columns))
    weight_wide = jnp.broadcast_to(band_weight[:, None], (every, columns))
    came = [(me + group - 2 * s) % group for s in range(1, chips)]
    where = [me, me ^ 1]
    for source in came:
        where += [source, source ^ 1]
    where = jnp.stack(where).astype(jnp.int32)

    def exchange(piece):
        far = [lax.ppermute(piece, "bins", s) for s in shifts]
        near = lax.ppermute(piece, "bins", partner)
        parts = [piece, near]
        for came_in in far:
            parts += [came_in, lax.ppermute(came_in, "bins", partner)]
        return parts

    whole = propagate(spectra, land_mask, speeds, 1)
    gathered = [[exchange(whole)]]
    spots, group_rows, over = plan(land_mask, chunks)
    groups = group_rows[:, 0]
    head, tail = edges(spectra, land_mask)
    before = lax.ppermute(tail, "space", [(n, n + 1) for n in range(slabs - 1)])
    after = lax.ppermute(head, "space", [(n + 1, n) for n in range(slabs - 1)])
    over = ballot(over)
    reach = 1
    while reach < slabs:
        ring = [(n, (n + reach) % slabs) for n in range(slabs)]
        over = jnp.maximum(over, lax.ppermute(over, "space", ring))
        reach *= 2

    for c, (blocks, packed) in enumerate(chunks[1:], 1):
        halos = (before, after) if 0 in blocks else None
        pieces = pack(spectra, land_mask, speeds, blocks, packed, groups, spots, halos)
        gathered.append([])
        for piece in pieces:
            gathered[c].append(exchange(piece))

    out = add_sources(where, gathered[0][0], kernels, growth_wide, weight_wide, land_mask, 1, None, spectra.shape)
    for c, (blocks, packed) in enumerate(chunks[1:], 1):
        parts = []
        for fields in gathered[c]:
            parts.append(packed_sources(where, fields, kernels, growth_wide, weight_wide))
            if 0 in blocks and len(parts) == len(packed) - 2:
                out = spread(parts, groups, spots, blocks[:-2], out)
            if 0 in blocks and len(parts) == len(packed) - 1:
                crowded, parts[-1] = lax.optimization_barrier((over[0, 0] > 0, parts[-1]))
                out = spread(parts, groups, spots, [0], out)
        if 0 in blocks:
            out = spread(parts[-2:], groups, spots, [last], out, sum(packed[:-2]))
        else:
            out = spread(parts, groups, spots, blocks, out)

    def again(out):
        def redo(block, out, halo=None, first=False):
            field = propagate(spectra, land_mask, speeds, block, halo, first, 1)
            fields = [field, lax.ppermute(field, "bins", partner)]
            for s in shifts:
                came_in = lax.ppermute(field, "bins", s)
                fields += [came_in, lax.ppermute(came_in, "bins", partner)]
            return add_sources(
                where, fields, kernels, growth_wide, weight_wide, land_mask, block, out, spectra.shape
            )

        out = lax.fori_loop(2, last, redo, out)
        return redo(last, redo(0, out, before, True), after)

    return lax.cond(crowded, again, lambda out: out, out)


def solution(mesh):
    in_specs = (P("bins", "space", None), P("space", None), P(), P(), P(), P())
    out_specs = P("bins", "space", None)
    return jax.shard_map(local, mesh=mesh, in_specs=in_specs, out_specs=out_specs, check_vma=False)
```
